256 devices in a mesh: grp: 2 (over core), gx: 16 (over y, z_lo), gy: 8 (over z_hi, x).
Axes of the slice: x: 4, y: 4, z: 8 (z_hi: 2, z_lo: 4; z = z_hi * 4 + z_lo), core: 2. Of those that a mesh axis runs over, the one named last changes fastest.
Arguments:
- source: float32 [128, 256, 256], P('gx', 'gy', 'grp'), may hold values from -8 to 8
- fill: int32 [128, 256, 256], P('gx', 'gy', 'grp'), may hold values 0 or 1
- material: int32 [128, 256, 256], P('gx', 'gy', 'grp'), may hold values from 0 to 7
- thickness: float32 [128, 256], P('gx', 'gy'), may hold values from 0.7 to 1.3
- perm_table: float32 [8], replicated, may hold values from 0.2 to 2
- stiff_table: float32 [8], replicated, may hold values from 0.5 to 2
Outputs:
- pressure: float32 [128, 256, 256], P('gx', 'gy', 'grp')
- displacement: float32 [128, 256, 256], P('gx', 'gy', 'grp')
- thickness_out: float32 [128, 256], P('gx', 'gy')
The draws below stay inside these ranges and needn't reach their ends.
All inputs are finite; a program needn't handle non-finite values. No bound on the sum of `fill` on one device may be relied on, other than what follows from the above.
Results may differ from the reference program's by a relative error of at most 0.0003.
Values sent between devices are 32-bit elements; how exact they have to be, the bound alone decides.
A program may use at most 128 MiB of HBM per device.

```python
import math
import jax
import jax.numpy as jnp
from jax import lax

ITERS = 8
STEPS = 2
MATS = 8
NX = 128
NY = 256
NZ = 256


def with_ends(drawn, key, least, largest):
    place = [jax.random.randint(jax.random.fold_in(key, axis), (), 0, length) for axis, length in enumerate(drawn.shape)]
    widest = drawn.shape.index(max(drawn.shape))
    next_to = place[:widest] + [(place[widest] + 1) % drawn.shape[widest]] + place[widest + 1:]
    return drawn.at[tuple(place)].set(least).at[tuple(next_to)].set(largest)


def shard_levels(rng, dims, shards, smallest, largest):
    def one(position, blocks):
        draws = jax.random.uniform(jax.random.fold_in(jax.random.fold_in(rng, 6), position), (blocks,), jnp.float32, smallest / len(shards), largest / len(shards))
        return jnp.repeat(jnp.exp(draws), dims[position] // blocks).reshape((-1,) + (1,) * (len(dims) - position - 1))

    loudness = one(*shards[0])
    for cut in shards[1:]:
        loudness = loudness * one(*cut)
    return loudness


def scatter_about(rng, extent, scale, most, split=(), held_as=jnp.bfloat16):
    entries = scale * jax.random.normal(rng, extent, jnp.float32)
    if split:
        entries = entries * shard_levels(rng, extent, split, -0.22, 0.18)
    return jnp.clip(entries, -most, most).astype(held_as)


def setup_inputs(seed: int = 0) -> dict:
    splits = jax.random.split(jax.random.key(seed), 7)
    return {
        "source": scatter_about(splits[0], (NX, NY, NZ), 2.0, 8.0, ((0, 16), (1, 8), (2, 2)), jnp.float32),
        "fill": with_ends((jax.random.randint(splits[1], (NX, NY, NZ), 0, 4) < 3).astype(jnp.int32), jax.random.fold_in(splits[1], 1), 0, 1),
        "material": with_ends(jax.random.randint(splits[2], (NX, NY, NZ), 0, MATS), jax.random.fold_in(splits[2], 1), 0, MATS - 1).astype(jnp.int32),
        "thickness": jnp.clip(0.7 + 0.59999996 * jax.random.uniform(splits[3], (NX, NY), jnp.float32) ** shard_levels(splits[3], (NX, NY), ((0, 16), (1, 8)), -0.2, 0.2), 0.7, 1.3),
        "perm_table": jnp.clip(jnp.exp(jax.random.uniform(splits[4], (MATS,), jnp.float32, math.log(0.2), math.log(2.0))), 0.2, 2.0),
        "stiff_table": jnp.clip(jnp.exp(jax.random.uniform(splits[5], (MATS,), jnp.float32, math.log(0.5), math.log(2.0))), 0.5, 2.0),
    }


def lookup(table, material):
    total = jnp.zeros(material.shape, jnp.float32)
    for entry in range(table.shape[0]):
        total = total + jnp.where(material == entry, table[entry], jnp.float32(0.0))
    return total

def neighbours(ext):
    return [ext[2:, 1:-1, 1:-1], ext[:-2, 1:-1, 1:-1], ext[1:-1, 2:, 1:-1], ext[1:-1, :-2, 1:-1], ext[1:-1, 1:-1, 2:], ext[1:-1, 1:-1, :-2]]

def face_terms(kext):
    centre = kext[1:-1, 1:-1, 1:-1]
    return [0.5 * (centre + side) for side in neighbours(kext)]

def relax(pext, faces, denom, fillf, source):
    total = source
    for face, side in zip(faces, neighbours(pext)):
        total = total + face * side
    return fillf * total / denom

def column_coeffs(stiffness):
    spad = jnp.pad(stiffness, ((0, 0), (0, 0), (1, 1)))
    upper = 0.5 * (stiffness + spad[:, :, 2:])
    lower = 0.5 * (stiffness + spad[:, :, :-2])
    cdiag = upper + lower + 0.001 * stiffness
    depth_pos = lax.broadcasted_iota(jnp.int32, stiffness.shape, 2)
    below = jnp.where(depth_pos == 0, jnp.zeros_like(lower), -lower)
    above = jnp.where(depth_pos == stiffness.shape[2] - 1, jnp.zeros_like(upper), -upper)
    return (below, cdiag, above)

def compact(load, coeffs):
    below, cdiag, above = coeffs
    rhs = (0.001 * load)[..., None]
    return lax.linalg.tridiagonal_solve(below, cdiag, above, rhs)[..., 0]

def reference(source, fill, material, thickness, perm_table, stiff_table):
    fillf = fill.astype(jnp.float32)
    conduct = lookup(perm_table, material)
    stiffness = lookup(stiff_table, material) * (1.0 - 0.5 * fillf)
    coeffs = column_coeffs(stiffness)
    pressure = jnp.zeros(source.shape, jnp.float32)
    disp = jnp.zeros(source.shape, jnp.float32)
    thick = thickness
    for step in range(STEPS):
        kvals = conduct * (thick * thick * thick)[:, :, None]
        faces = face_terms(jnp.pad(kvals, 1))
        denom = sum(faces) + 1.0 - fillf
        for sweep in range(ITERS):
            pressure = relax(jnp.pad(pressure, 1), faces, denom, fillf, source)
        disp = compact(1.0 - pressure, coeffs)
        comp = jnp.mean(disp, axis=2)
        thick = thick * (1.0 + 0.3 * jnp.tanh(comp))
    return (pressure, disp, thick)
```

```python
import jax
import jax.numpy as jnp
from jax import lax
from jax.experimental import pallas as pl
from jax.experimental.pallas import tpu as pltpu
from jax.sharding import PartitionSpec as P

STEPS = 2
W = 4
MESH = pl.DeviceIdType.MESH
DIRS = [(-1, -1), (-1, 0), (-1, 1), (0, -1), (0, 1), (1, -1), (1, 0), (1, 1)]
UNROLL = 2


def spread(table, material, count):
    total = jnp.zeros(material.shape, jnp.float32)
    for entry in range(count):
        total = jnp.where(material == entry, table[entry], total)
    return total


def make_kernel(nx, ny, nz, ngx, ngy, mats):
    rows, depth = ny // 2, 2 * nz
    ex, ey = nx + 2 * W, rows + 2 * W
    nslab = 2 * ngy
    levels = depth.bit_length() - 1
    x_from = {-1: (W, W), 0: (W, nx), 1: (nx, W)}
    x_to = {-1: (W + nx, W), 0: (W, nx), 1: (0, W)}
    y_from = {-1: (0, W), 0: (0, rows), 1: (rows - W, W)}
    y_to = {-1: (rows, W), 0: (0, rows), 1: (rows + W, W)}

    def kernel(source, fill, material, thickness, perm, stiffs, p_out, d_out, th_out,
               s_ext, f_ext, k_ext, px0, px1, px2, ta, tb, mat, gx_, gy_, gz_, a_,
               alpha, gamma, inv, wts, cols, fin_p, fin_d, fin_t,
               send, recv, psend, precv, loc):
        g = lax.axis_index("grp")
        ix = lax.axis_index("gx")
        slab = 2 * lax.axis_index("gy") + g
        other = 1 - g

        def place(dx, dy):
            x = jnp.clip(ix + dx, 0, ngx - 1)
            s = jnp.clip(slab + dy, 0, nslab - 1)
            return {"grp": lax.rem(s, 2), "gx": x, "gy": lax.div(s, 2)}

        def there(dx, dy):
            ok = jnp.int32(1)
            if dx == -1:
                ok = ok * jnp.where(ix > 0, 1, 0)
            if dx == 1:
                ok = ok * jnp.where(ix < ngx - 1, 1, 0)
            if dy == -1:
                ok = ok * jnp.where(slab > 0, 1, 0)
            if dy == 1:
                ok = ok * jnp.where(slab < nslab - 1, 1, 0)
            return ok

        alive = [there(*d) for d in DIRS]

        barrier = pltpu.get_barrier_semaphore()
        for i, d in enumerate(DIRS):
            @pl.when(alive[i] == 1)
            def _():
                pl.semaphore_signal(barrier, 1, device_id=place(*d), device_id_type=MESH)
        pl.semaphore_wait(barrier, sum(alive))

        mine = pl.multiple_of(g * rows, rows)
        theirs = pl.multiple_of(other * rows, rows)
        z_here = pl.multiple_of(g * nz, nz)
        z_there = pl.multiple_of(other * nz, nz)
        own_x, own_y = pl.ds(W, nx), pl.ds(0, rows)

        def trade(n, ref, dst):
            out = pltpu.make_async_remote_copy(
                ref.at[:, pl.ds(theirs, rows), :], dst.at[own_x, own_y, pl.ds(z_here, nz)],
                psend.at[n], precv.at[n], device_id={"grp": other}, device_id_type=MESH)
            keep = pltpu.make_async_copy(
                ref.at[:, pl.ds(mine, rows), :], dst.at[own_x, own_y, pl.ds(z_here, nz)], loc.at[n])
            return out, keep

        trades = [trade(0, source, s_ext), trade(1, fill, f_ext), trade(2, material, mat)]
        for out, keep in trades:
            out.start()
            keep.start()

        def hop(e, ref, i):
            dx, dy = DIRS[i]
            if ref is cols:
                src = ref.at[1, pl.ds(*y_from[dy]), :]
                dst = ref.at[1 - dx, pl.ds(*y_to[dy]), :]
            else:
                src = ref.at[pl.ds(*x_from[dx]), pl.ds(*y_from[dy]), :]
                dst = ref.at[pl.ds(*x_to[dx]), pl.ds(*y_to[dy]), :]
            return pltpu.make_async_remote_copy(
                src, dst, send.at[e, i], recv.at[e, i], device_id=place(dx, dy), device_id_type=MESH)

        def push(e, ref):
            for i in range(8):
                @pl.when(alive[i] == 1)
                def _():
                    hop(e, ref, i).start()

        def arrive(e, ref):
            for i in range(8):
                @pl.when(alive[7 - i] == 1)
                def _():
                    hop(e, ref, i).wait_recv()

        def sent(e, ref):
            for i in range(8):
                @pl.when(alive[i] == 1)
                def _():
                    hop(e, ref, i).wait_send()

        lane = lax.broadcasted_iota(jnp.int32, (rows, 128), 1)
        pick_row = lax.broadcasted_iota(jnp.int32, (rows, ny), 1) == (
            lax.broadcasted_iota(jnp.int32, (rows, ny), 0) + g * rows)

        def column_of(x):
            line = jnp.broadcast_to(thickness[pl.ds(x, 1), :], (rows, ny))
            return jnp.sum(jnp.where(pick_row, line, 0.0), axis=1, keepdims=True)

        th = jnp.zeros((rows, 128), jnp.float32)
        for x in range(nx):
            th = jnp.where(lane == x, column_of(x), th)

        for n, ref in ((0, s_ext), (1, f_ext)):
            trades[n][0].wait_recv()
            trades[n][1].wait()
            push(n, ref)
        trades[2][0].wait_recv()
        trades[2][1].wait()

        for x in range(nx):
            t = th[:, x:x + 1]
            k_ext[W + x, 0:rows, :] = spread(perm, mat[W + x, 0:rows, :], mats) * (t * t * t)
        push(2, k_ext)

        for i in range(8):
            dx, dy = DIRS[i]
            x0, xn = x_to[-dx]
            y0, yn = y_to[-dy]

            @pl.when(alive[i] == 0)
            def _():
                s_ext[x0:x0 + xn, y0:y0 + yn, :] = jnp.zeros((xn, yn, depth), jnp.float32)
                f_ext[x0:x0 + xn, y0:y0 + yn, :] = jnp.zeros((xn, yn, depth), jnp.int32)
                k_ext[x0:x0 + xn, y0:y0 + yn, :] = jnp.zeros((xn, yn, depth), jnp.float32)
                for ref in (px0, px1, px2):
                    ref[x0:x0 + xn, y0:y0 + yn, :] = jnp.zeros((xn, yn, depth), jnp.float32)
                cols[1 + dx, y0:y0 + yn, :] = jnp.zeros((yn, 128), jnp.float32)

        zpos = lax.broadcasted_iota(jnp.int32, (rows, depth), 1)

        def reduce_columns(x, carry):
            fl = f_ext[W + x, 0:rows, :].astype(jnp.float32)
            st = spread(stiffs, mat[W + x, 0:rows, :], mats) * (1.0 - 0.5 * fl)
            low = jnp.where(zpos == 0, 0.0, pltpu.roll(st, 1, 1))
            high = jnp.where(zpos == depth - 1, 0.0, pltpu.roll(st, depth - 1, 1))
            up = 0.5 * (st + high)
            down = 0.5 * (st + low)
            a = jnp.where(zpos == 0, 0.0, down)
            c = jnp.where(zpos == depth - 1, 0.0, up)
            e = 0.001 * st + jnp.where(zpos == 0, down, 0.0) + jnp.where(zpos == depth - 1, up, 0.0)
            r = jnp.full((rows, depth), 0.001 / depth, jnp.float32)
            for level in range(levels):
                stride = 1 << level
                back = depth - stride
                recip = 1.0 / (a + c + e)
                al = a * pltpu.roll(recip, stride, 1)
                ga = c * pltpu.roll(recip, back, 1)
                alpha[level, x] = al
                gamma[level, x] = ga
                a = al * pltpu.roll(a, stride, 1)
                c = ga * pltpu.roll(c, back, 1)
                e = e + al * pltpu.roll(e, stride, 1) + ga * pltpu.roll(e, back, 1)
                r = r + al * pltpu.roll(r, stride, 1) + ga * pltpu.roll(r, back, 1)
            recip = 1.0 / e
            inv[x] = recip
            wts[x] = r * recip
            return carry

        lax.fori_loop(0, nx, reduce_columns, 0)

        zfull = lax.broadcasted_iota(jnp.int32, (ey, depth), 1)

        def faces(x, carry):
            k = k_ext[x]
            front = jnp.where(zfull == 0, 0.0, pltpu.roll(k, 1, 1))
            back = jnp.where(zfull == depth - 1, 0.0, pltpu.roll(k, depth - 1, 1))
            gzp = 0.5 * (k + back)
            gzm = 0.5 * (k + front)
            gyp = 0.5 * (k + pltpu.roll(k, ey - 1, 0))
            gym = 0.5 * (k + pltpu.roll(k, 1, 0))
            gxp = 0.5 * (k + k_ext[x + 1])
            gxm = 0.5 * (k + k_ext[x - 1])
            fl = f_ext[x].astype(jnp.float32)
            denom = gxp + gxm + gyp + gym + gzp + gzm + 1.0 - fl
            gx_[x] = gxp
            gy_[x] = gyp
            gz_[x] = jnp.where(zfull == depth - 1, 0.0, gzp)
            a_[x] = fl / denom
            return carry

        def all_faces():
            gx_[0] = 0.5 * (k_ext[0] + k_ext[1])
            lax.fori_loop(1, ex - 1, faces, 0)

        def relax(src, dst, level, width):
            def one(x, carry):
                here = src[x]
                gy = gy_[x]
                gz = gz_[x]
                total = s_ext[x] + gx_[x] * src[x + 1] + gx_[x - 1] * src[x - 1]
                total = total + gy * pltpu.roll(here, ey - 1, 0) + pltpu.roll(gy * here, 1, 0)
                total = total + gz * pltpu.roll(here, depth - 1, 1) + pltpu.roll(gz * here, 1, 1)
                value = a_[x] * total
                if width == ey:
                    dst[x] = value
                elif dst is fin_p:
                    dst[x - W] = value[0:width]
                else:
                    dst[x, 0:width] = value[0:width]
                return carry

            lax.fori_loop(level, ex - level, one, 0, unroll=UNROLL)

        def first(x, carry):
            ta[x] = a_[x] * s_ext[x]
            return carry

        def mean_factor(held, base):
            comp = jnp.zeros((rows, 128), jnp.float32)
            for x in range(nx):
                part = wts[x] * (1.0 - held[base + x, 0:rows, :])
                comp = jnp.where(lane == x, jnp.sum(part, axis=1, keepdims=True), comp)
            return 1.0 + 0.3 * jnp.tanh(comp)

        arrive(2, k_ext)
        arrive(1, f_ext)
        all_faces()
        arrive(0, s_ext)
        lax.fori_loop(1, ex - 1, first, 0)
        relax(ta, tb, 2, ey)
        relax(tb, ta, 3, ey)
        relax(ta, px0, 4, rows)
        push(3, px0)
        arrive(3, px0)
        relax(px0, ta, 1, ey)
        relax(ta, tb, 2, ey)
        relax(tb, ta, 3, ey)
        relax(ta, px1, 4, rows)

        factor = mean_factor(px1, W)
        cols[1, 0:rows, :] = factor
        push(5, cols)
        push(4, px1)
        th = th * factor
        arrive(5, cols)
        sent(2, k_ext)
        for x in range(ex):
            part, pos = (0, x + nx - W) if x < W else ((1, x - W) if x < W + nx else (2, x - W - nx))
            t = cols[part, :, pos:pos + 1]
            k_ext[x] = k_ext[x] * (t * t * t)
        all_faces()
        arrive(4, px1)
        relax(px1, ta, 1, ey)
        relax(ta, tb, 2, ey)
        relax(tb, ta, 3, ey)
        relax(ta, px2, 4, rows)
        push(6, px2)
        arrive(6, px2)
        relax(px2, ta, 1, ey)
        relax(ta, tb, 2, ey)
        relax(tb, ta, 3, ey)
        relax(ta, fin_p, 4, rows)

        def give(n, ref, dst):
            out = pltpu.make_async_remote_copy(
                ref.at[:, :, pl.ds(z_there, nz)], dst.at[:, pl.ds(mine, rows), :],
                psend.at[n], precv.at[n], device_id={"grp": other}, device_id_type=MESH)
            keep = pltpu.make_async_copy(
                ref.at[:, :, pl.ds(z_here, nz)], dst.at[:, pl.ds(mine, rows), :], loc.at[n])
            return out, keep

        gives = [give(3, fin_p, p_out), give(4, fin_d, d_out)]
        for c in gives[0]:
            c.start()

        def solve_columns(x, carry):
            r = 0.001 * (1.0 - fin_p[x])
            for level in range(levels):
                stride = 1 << level
                r = (r + alpha[level, x] * pltpu.roll(r, stride, 1)
                     + gamma[level, x] * pltpu.roll(r, depth - stride, 1))
            fin_d[x] = r * inv[x]
            return carry

        lax.fori_loop(0, nx, solve_columns, 0, unroll=2)
        for c in gives[1]:
            c.start()
        fin_t[...] = th * mean_factor(fin_p, 0)
        t_out = pltpu.make_async_remote_copy(
            fin_t, th_out.at[pl.ds(mine, rows), :], psend.at[5], precv.at[5],
            device_id={"grp": other}, device_id_type=MESH)
        t_keep = pltpu.make_async_copy(fin_t, th_out.at[pl.ds(mine, rows), :], loc.at[5])
        t_out.start()
        t_keep.start()

        for e, ref in ((0, s_ext), (1, f_ext), (3, px0), (4, px1), (5, cols), (6, px2)):
            sent(e, ref)
        for out, keep in trades:
            out.wait_send()
        for out, keep in gives + [(t_out, t_keep)]:
            out.wait_send()
            out.wait_recv()
            keep.wait()

    return kernel, rows, depth, ex, ey, levels


def body(source, fill, material, thickness, perm_table, stiff_table):
    nx, ny, nz = source.shape
    kernel, rows, depth, ex, ey, levels = make_kernel(
        nx, ny, nz, lax.axis_size("gx"), lax.axis_size("gy"), perm_table.shape[0])
    f32, i32 = jnp.float32, jnp.int32
    vm, sm = pl.BlockSpec(memory_space=pltpu.VMEM), pl.BlockSpec(memory_space=pltpu.SMEM)
    ext = pltpu.VMEM((ex, ey, depth), f32)
    iext = pltpu.VMEM((ex, ey, depth), i32)
    own = pltpu.VMEM((nx, rows, depth), f32)
    pressure, disp, thick = pl.pallas_call(
        kernel,
        out_shape=(
            jax.ShapeDtypeStruct((nx, ny, nz), f32),
            jax.ShapeDtypeStruct((nx, ny, nz), f32),
            jax.ShapeDtypeStruct((ny, 128), f32),
        ),
        in_specs=[vm, vm, vm, vm, sm, sm],
        out_specs=(vm, vm, vm),
        scratch_shapes=[
            ext, iext, ext, ext, ext, ext, ext, ext, iext, ext, ext, ext, ext,
            pltpu.VMEM((levels, nx, rows, depth), f32),
            pltpu.VMEM((levels, nx, rows, depth), f32),
            own, own,
            pltpu.VMEM((3, ey, 128), f32),
            own, own,
            pltpu.VMEM((rows, 128), f32),
            pltpu.SemaphoreType.DMA((7, 8)),
            pltpu.SemaphoreType.DMA((7, 8)),
            pltpu.SemaphoreType.DMA((6,)),
            pltpu.SemaphoreType.DMA((6,)),
            pltpu.SemaphoreType.DMA((6,)),
        ],
        compiler_params=pltpu.CompilerParams(collective_id=0, has_side_effects=True),
    )(source, fill, material, thickness, perm_table, stiff_table)
    return pressure, disp, thick[:, :nx].T


def solution(mesh):
    return jax.shard_map(
        body,
        mesh=mesh,
        in_specs=(
            P("gx", "gy", "grp"),
            P("gx", "gy", "grp"),
            P("gx", "gy", "grp"),
            P("gx", "gy"),
            P(),
            P(),
        ),
        out_specs=(P("gx", "gy", "grp"), P("gx", "gy", "grp"), P("gx", "gy")),
        check_vma=False,
    )
```

```python
import jax
import jax.numpy as jnp
from jax import lax
from jax.experimental import pallas as pl
from jax.experimental.pallas import tpu as pltpu
from jax.sharding import PartitionSpec as P

W = 4
VMEM_LIMIT = 24 << 20
MESH = pl.DeviceIdType.MESH
DIRS = [(-1, -1), (-1, 0), (-1, 1), (0, -1), (0, 1), (1, -1), (1, 0), (1, 1)]
NINE = [(0, 0)] + DIRS
ORDER = [0, 1, 2, 3, 4, 5, 6, 7]
FACES = 2


def spread(table, material, count):
    total = jnp.zeros(material.shape, jnp.float32)
    for entry in range(count):
        total = jnp.where(material == entry, table[entry], total)
    return total


def make_kernel(nx, ny, nz, ngx, ngy, mats):
    rows, depth = ny // 2, 2 * nz
    ex, ey = nx + 2 * W, rows + 2 * W
    nslab = 2 * ngy
    levels = depth.bit_length() - 1

    def blocks(dx, dy, reach):
        xr = reach - abs(dy)
        yr = reach - abs(dx)
        xs, xd = {-1: ((0, xr), (W + nx, xr)), 0: ((0, nx), (W, nx)), 1: ((nx - xr, xr), (W - xr, xr))}[dx]
        ys, yd = {-1: ((0, yr), (rows, yr)), 0: ((0, rows), (0, rows)),
                  1: ((rows - yr, yr), (ey - yr, yr))}[dy]
        return xs, ys, xd, yd

    def kernel(source, fill, material, thickness, perm_table, stiff_table, p_out, d_out, th_out,
               s_ext, f_ext, k_ext, px0, px1, px2, ta, tb, gx_, gy_, gz_, a_,
               alpha, gamma, inv, wts, cols, fin_p, fin_d, mat, kloc, stloc, st, thick, line, line_in, perm, stiffs,
               csend, crecv, cloc, send, recv, psend, precv, loc):
        g = lax.axis_index("grp")
        ix = lax.axis_index("gx")
        iy = lax.axis_index("gy")
        slab = 2 * iy + g
        other = 1 - g

        def within(value, count):
            return jnp.where(value >= 0, 1, 0) * jnp.where(value < count, 1, 0)

        def place(dx, dy):
            x = jnp.clip(ix + dx, 0, ngx - 1)
            s = jnp.clip(slab + dy, 0, nslab - 1)
            return {"grp": lax.rem(s, 2), "gx": x, "gy": lax.div(s, 2)}

        alive = [within(ix + dx, ngx) * within(slab + dy, nslab) for dx, dy in DIRS]

        barrier = pltpu.get_barrier_semaphore()
        for dx in (-1, 0, 1):
            for dgy in (0, 2 * g - 1):
                for core in range(2):
                    ok = within(ix + dx, ngx) * within(iy + dgy, ngy)
                    if dx == 0 and isinstance(dgy, int):
                        ok = jnp.where(g == core, 0, 1)

                    @pl.when(ok == 1)
                    def _():
                        target = {"grp": core, "gx": jnp.clip(ix + dx, 0, ngx - 1),
                                  "gy": jnp.clip(iy + dgy, 0, ngy - 1)}
                        pl.semaphore_signal(barrier, 1, device_id=target, device_id_type=MESH)
        greeted = (sum(within(ix + dx, ngx) for dx in (-1, 0, 1))
                   * sum(within(2 * iy + j, nslab) for j in (-1, 0, 1, 2)) - 1)

        load_th = pltpu.make_async_copy(thickness, thick, loc.at[0])
        load_mat = pltpu.make_async_copy(material, mat, loc.at[1])
        load_perm = pltpu.make_async_copy(perm_table, perm, loc.at[6])
        load_stiff = pltpu.make_async_copy(stiff_table, stiffs, loc.at[7])
        for c in (load_th, load_mat, load_perm, load_stiff):
            c.start()

        for i in range(8):
            dx, dy = DIRS[i]
            _, _, (x0, xn), (y0, yn) = blocks(-dx, -dy, W)

            @pl.when(alive[i] == 0)
            def _():
                s_ext[x0:x0 + xn, y0:y0 + yn, :] = jnp.zeros((xn, yn, depth), jnp.float32)
                f_ext[x0:x0 + xn, y0:y0 + yn, :] = jnp.zeros((xn, yn, depth), jnp.int32)
                k_ext[x0:x0 + xn, y0:y0 + yn, :] = jnp.zeros((xn, yn, depth), jnp.float32)
                for ref in (px0, px1, px2):
                    ref[x0:x0 + xn, y0:y0 + yn, :] = jnp.zeros((xn, yn, depth), jnp.float32)
                cols[1 + dx, y0:y0 + yn, :] = jnp.zeros((yn, 128), jnp.float32)

        for c in (load_th, load_mat, load_perm, load_stiff):
            c.wait()
        diagonal = lax.broadcasted_iota(jnp.int32, (ny, ny), 0) == lax.broadcasted_iota(jnp.int32, (ny, ny), 1)
        for x in range(nx):
            across = jnp.broadcast_to(thick[x:x + 1, :], (ny, ny))
            t = jnp.sum(jnp.where(diagonal, across, 0.0), axis=1, keepdims=True)
            m = mat[x]
            kloc[x] = spread(perm, m, mats) * (t * t * t)
            stloc[x] = spread(stiffs, m, mats)

        pl.semaphore_wait(barrier, greeted)

        mine = pl.multiple_of(g * rows, rows)
        theirs = pl.multiple_of(other * rows, rows)
        z_here = pl.multiple_of(g * nz, nz)
        z_there = pl.multiple_of(other * nz, nz)
        consts = [(0, kloc, k_ext, W), (1, fill, f_ext, W - 1), (2, source, s_ext, W - 1)]

        def const_send(n, v, i, local=False):
            _, src, ext, reach = consts[n]
            dx, dy = NINE[i]
            (xs, xn), (ys, yn), (xd, _), (yd, _) = blocks(dx, dy, reach)
            core, dgy = (v + dy) % 2, (v + dy) // 2
            from_ = src.at[pl.ds(xs, xn), pl.ds(v * rows + ys, yn), :]
            to = ext.at[pl.ds(xd, xn), pl.ds(yd, yn), pl.ds(z_here, nz)]
            target = {"grp": core, "gx": jnp.clip(ix + dx, 0, ngx - 1), "gy": jnp.clip(iy + dgy, 0, ngy - 1)}
            if local:
                return pltpu.make_async_copy(from_, to, cloc.at[n, 0 if dy == 0 else 1])
            return pltpu.make_async_remote_copy(
                from_, to, csend.at[n, v, i], crecv.at[n, g, i], device_id=target, device_id_type=MESH)

        def const_each(group, do_away, do_keep):
            for v in range(2):
                for i in range(9):
                    dx, dy = NINE[i]
                    core, dgy = (v + dy) % 2, (v + dy) // 2
                    ok = within(ix + dx, ngx) * within(iy + dgy, ngy)
                    if dx == 0 and dgy == 0:
                        ok = jnp.where(g == core, 0, 1)
                        if do_keep is not None:
                            @pl.when(g == core)
                            def _():
                                for n in group:
                                    do_keep(const_send(n, v, i, True))

                    @pl.when(ok == 1)
                    def _():
                        for n in group:
                            do_away(const_send(n, v, i))

        def const_arrive(group):
            for src in range(2):
                for i in range(9):
                    dx, dy = NINE[i]
                    ok = within(ix - dx, ngx) * within(slab - dy, nslab)
                    if dx == 0:
                        here = jnp.where(g == src, 1, 0)
                        if dy == 1:
                            here = here * g
                        if dy == -1:
                            here = here * other
                        ok = ok * (1 - here)

                        @pl.when(here == 1)
                        def _():
                            for n in group:
                                _, ref, ext, reach = consts[n]
                                (xs, xn), (ys, yn), (xd, _), (yd, _) = blocks(dx, dy, reach)
                                pltpu.make_async_copy(
                                    ref.at[pl.ds(xs, xn), pl.ds(ys, yn), :],
                                    ext.at[pl.ds(xd, xn), pl.ds(yd, yn), pl.ds(src * nz, nz)],
                                    cloc.at[n, 0 if dy == 0 else 1]).wait()

                    @pl.when(ok == 1)
                    def _():
                        for n in group:
                            _, ref, ext, reach = consts[n]
                            (xs, xn), (ys, yn), (xd, _), (yd, _) = blocks(dx, dy, reach)
                            pltpu.make_async_remote_copy(
                                ref.at[pl.ds(xs, xn), pl.ds(ys, yn), :],
                                ext.at[pl.ds(xd, xn), pl.ds(yd, yn), pl.ds(src * nz, nz)],
                                csend.at[n, 0, i], crecv.at[n, src, i],
                                device_id={"grp": other}, device_id_type=MESH).wait_recv()

        st_away = pltpu.make_async_remote_copy(
            stloc.at[:, pl.ds(theirs, rows), :], st.at[:, :, pl.ds(z_here, nz)],
            psend.at[0], precv.at[0], device_id={"grp": other}, device_id_type=MESH)
        st_keep = pltpu.make_async_copy(
            stloc.at[:, pl.ds(mine, rows), :], st.at[:, :, pl.ds(z_here, nz)], loc.at[2])
        st_away.start()
        st_keep.start()
        for group in ((0, 1), (2,)):
            const_each(group, lambda c: c.start(), lambda c: c.start())

        def hop(e, ref, i):
            dx, dy = DIRS[i]
            (xs, xn), (ys, yn), (xd, _), (yd, _) = blocks(dx, dy, W)
            if ref is cols:
                src = ref.at[1, pl.ds(ys, yn), :]
                dst = ref.at[1 - dx, pl.ds(yd, yn), :]
            else:
                src = ref.at[pl.ds(W + xs, xn), pl.ds(ys, yn), :]
                dst = ref.at[pl.ds(xd, xn), pl.ds(yd, yn), :]
            return pltpu.make_async_remote_copy(
                src, dst, send.at[e, i], recv.at[e, i], device_id=place(dx, dy), device_id_type=MESH)

        def push(e, ref):
            for i in ORDER:
                @pl.when(alive[i] == 1)
                def _():
                    hop(e, ref, i).start()

        def arrive(e, ref):
            for i in range(8):
                @pl.when(alive[7 - i] == 1)
                def _():
                    hop(e, ref, i).wait_recv()

        def sent(e, ref):
            for i in range(8):
                @pl.when(alive[i] == 1)
                def _():
                    hop(e, ref, i).wait_send()

        zpos = lax.broadcasted_iota(jnp.int32, (rows, depth), 1)

        def reduce_columns(x, carry):
            s = st[x] * (1.0 - 0.5 * f_ext[W + x, 0:rows, :].astype(jnp.float32))
            low = jnp.where(zpos == 0, 0.0, pltpu.roll(s, 1, 1))
            high = jnp.where(zpos == depth - 1, 0.0, pltpu.roll(s, depth - 1, 1))
            up = 0.5 * (s + high)
            down = 0.5 * (s + low)
            a = jnp.where(zpos == 0, 0.0, down)
            c = jnp.where(zpos == depth - 1, 0.0, up)
            e = 0.001 * s + jnp.where(zpos == 0, down, 0.0) + jnp.where(zpos == depth - 1, up, 0.0)
            r = jnp.full((rows, depth), 0.001 / depth, jnp.float32)
            for level in range(levels):
                stride = 1 << level
                back = depth - stride
                recip = 1.0 / (a + c + e)
                al = a * pltpu.roll(recip, stride, 1)
                ga = c * pltpu.roll(recip, back, 1)
                alpha[level, x] = al
                gamma[level, x] = ga
                a = al * pltpu.roll(a, stride, 1)
                c = ga * pltpu.roll(c, back, 1)
                e = e + al * pltpu.roll(e, stride, 1) + ga * pltpu.roll(e, back, 1)
                r = r + al * pltpu.roll(r, stride, 1) + ga * pltpu.roll(r, back, 1)
            recip = 1.0 / e
            inv[x] = recip
            wts[x] = r * recip
            return carry

        zfull = lax.broadcasted_iota(jnp.int32, (ey, depth), 1)

        def faces(x, carry):
            k = k_ext[x]
            front = jnp.where(zfull == 0, 0.0, pltpu.roll(k, 1, 1))
            back = jnp.where(zfull == depth - 1, 0.0, pltpu.roll(k, depth - 1, 1))
            gzp = 0.5 * (k + back)
            gzm = 0.5 * (k + front)
            gyp = 0.5 * (k + pltpu.roll(k, ey - 1, 0))
            gym = 0.5 * (k + pltpu.roll(k, 1, 0))
            gxp = 0.5 * (k + k_ext[x + 1])
            gxm = 0.5 * (k + k_ext[x - 1])
            fl = f_ext[x].astype(jnp.float32)
            denom = gxp + gxm + gyp + gym + gzp + gzm + 1.0 - fl
            gx_[x] = gxp
            gy_[x] = gyp
            gz_[x] = jnp.where(zfull == depth - 1, 0.0, gzp)
            a_[x] = fl / denom
            return carry

        def all_faces():
            gx_[0] = 0.5 * (k_ext[0] + k_ext[1])
            lax.fori_loop(1, ex - 1, faces, 0, unroll=FACES)

        def relax(src, dst, level, width):
            def one(x, carry):
                here = src[x]
                gy = gy_[x]
                gz = gz_[x]
                total = s_ext[x] + gx_[x] * src[x + 1] + gx_[x - 1] * src[x - 1]
                total = total + gy * pltpu.roll(here, ey - 1, 0) + pltpu.roll(gy * here, 1, 0)
                total = total + gz * pltpu.roll(here, depth - 1, 1) + pltpu.roll(gz * here, 1, 1)
                value = a_[x] * total
                if width == ey:
                    dst[x] = value
                elif dst is fin_p:
                    dst[x - W] = value[0:width]
                else:
                    dst[x, 0:width] = value[0:width]
                return carry

            lax.fori_loop(level, ex - level, one, 0, unroll=ex - 2 * level)

        def first(x, carry):
            ta[x] = a_[x] * s_ext[x]
            return carry

        lane = lax.broadcasted_iota(jnp.int32, (rows, 128), 1)

        def mean_factor(held, base):
            comp = jnp.zeros((rows, 128), jnp.float32)
            for x in range(nx):
                part = wts[x] * (1.0 - held[base + x, 0:rows, :])
                comp = jnp.where(lane == x, jnp.sum(part, axis=1, keepdims=True), comp)
            return 1.0 + 0.3 * jnp.tanh(comp)

        st_away.wait_recv()
        st_keep.wait()
        const_arrive((0, 1))
        all_faces()
        const_arrive((2,))
        lax.fori_loop(1, ex - 1, first, 0, unroll=2)
        relax(ta, tb, 2, ey)
        relax(tb, ta, 3, ey)
        relax(ta, px0, 4, rows)
        push(0, px0)
        lax.fori_loop(0, nx, reduce_columns, 0)
        for group in ((0, 1), (2,)):
            const_each(group, lambda c: c.wait_send(), None)
        st_away.wait_send()
        arrive(0, px0)
        relax(px0, ta, 1, ey)
        relax(ta, tb, 2, ey)
        relax(tb, ta, 3, ey)
        relax(ta, px1, 4, rows)

        factor = mean_factor(px1, W)
        cols[1, 0:rows, :] = factor
        push(2, cols)
        push(1, px1)
        sent(0, px0)
        arrive(2, cols)
        for x in range(ex):
            part, pos = (0, x + nx - W) if x < W else ((1, x - W) if x < W + nx else (2, x - W - nx))
            t = cols[part, :, pos:pos + 1]
            k_ext[x] = k_ext[x] * (t * t * t)
        all_faces()
        arrive(1, px1)
        relax(px1, ta, 1, ey)
        relax(ta, tb, 2, ey)
        relax(tb, ta, 3, ey)
        relax(ta, px2, 4, rows)
        push(3, px2)
        sent(2, cols)
        sent(1, px1)
        arrive(3, px2)
        relax(px2, ta, 1, ey)
        relax(ta, tb, 2, ey)
        relax(tb, ta, 3, ey)
        relax(ta, fin_p, 4, rows)

        def give(n, ref, dst, x0, xn):
            out = pltpu.make_async_remote_copy(
                ref.at[pl.ds(x0, xn), :, pl.ds(z_there, nz)], dst.at[pl.ds(x0, xn), pl.ds(mine, rows), :],
                psend.at[n], precv.at[n], device_id={"grp": other}, device_id_type=MESH)
            keep = pltpu.make_async_copy(
                ref.at[pl.ds(x0, xn), :, pl.ds(z_here, nz)], dst.at[pl.ds(x0, xn), pl.ds(mine, rows), :],
                loc.at[2 + n])
            return out, keep

        half = nx // 2
        gives = [give(1, fin_p, p_out, 0, nx), give(2, fin_d, d_out, 0, half), give(3, fin_d, d_out, half, half)]
        for c in gives[0]:
            c.start()

        def solve_columns(x, carry):
            r = 0.001 * (1.0 - fin_p[x])
            for level in range(levels):
                stride = 1 << level
                r = (r + alpha[level, x] * pltpu.roll(r, stride, 1)
                     + gamma[level, x] * pltpu.roll(r, depth - stride, 1))
            fin_d[x] = r * inv[x]
            return carry

        for n in range(2):
            lax.fori_loop(n * half, (n + 1) * half, solve_columns, 0, unroll=half)
            for c in gives[1 + n]:
                c.start()

        factor = factor * mean_factor(fin_p, 0)
        spot = lane == lax.broadcasted_iota(jnp.int32, (rows, 128), 0) + g * rows
        pick = lax.broadcasted_iota(jnp.int32, (nx, 128), 0)
        mixed = jnp.zeros((nx, 128), jnp.float32)
        for x in range(nx):
            row = jnp.sum(jnp.where(spot, factor[:, x:x + 1], 0.0), axis=0, keepdims=True)
            mixed = jnp.where(pick == x, row, mixed)
        line[...] = mixed
        t_out = pltpu.make_async_remote_copy(
            line, line_in, psend.at[4], precv.at[4], device_id={"grp": other}, device_id_type=MESH)
        t_out.start()
        sent(3, px2)
        for out, keep in gives:
            out.wait_send()
            keep.wait()
        t_out.wait_send()
        t_out.wait_recv()
        th_out[...] = thick[...] * (mixed + line_in[...])[:, 0:ny]
        for out, keep in gives:
            out.wait_recv()

    return kernel, rows, depth, ex, ey, levels


def body(source, fill, material, thickness, perm_table, stiff_table):
    nx, ny, nz = source.shape
    kernel, rows, depth, ex, ey, levels = make_kernel(
        nx, ny, nz, lax.axis_size("gx"), lax.axis_size("gy"), perm_table.shape[0])
    f32, i32 = jnp.float32, jnp.int32
    vm = pl.BlockSpec(memory_space=pltpu.VMEM)
    hb = pl.BlockSpec(memory_space=pl.ANY)
    hbm = pl.BlockSpec(memory_space=pltpu.HBM)
    ext = pltpu.VMEM((ex, ey, depth), f32)
    iext = pltpu.VMEM((ex, ey, depth), i32)
    own = pltpu.VMEM((nx, rows, depth), f32)
    brick = pltpu.VMEM((nx, ny, nz), f32)
    dma = pltpu.SemaphoreType.DMA
    return pl.pallas_call(
        kernel,
        out_shape=(
            jax.ShapeDtypeStruct((nx, ny, nz), f32),
            jax.ShapeDtypeStruct((nx, ny, nz), f32),
            jax.ShapeDtypeStruct((nx, ny), f32),
        ),
        in_specs=[hbm] * 6,
        out_specs=(hb, hb, vm),
        scratch_shapes=[
            ext, iext, ext, ext, ext, ext, ext, ext, ext, ext, ext, ext,
            pltpu.VMEM((levels, nx, rows, depth), f32),
            pltpu.VMEM((levels, nx, rows, depth), f32),
            own, own,
            pltpu.VMEM((3, ey, 128), f32),
            own, own,
            pltpu.VMEM((nx, ny, nz), i32), brick, brick, own,
            pltpu.VMEM((nx, ny), f32),
            pltpu.VMEM((nx, 128), f32),
            pltpu.VMEM((nx, 128), f32),
            pltpu.SMEM(perm_table.shape, f32), pltpu.SMEM(stiff_table.shape, f32),
            dma((3, 2, 9)), dma((3, 2, 9)), dma((3, 2)),
            dma((4, 8)), dma((4, 8)), dma((5,)), dma((5,)), dma((8,)),
        ],
        compiler_params=pltpu.CompilerParams(
            collective_id=0, has_side_effects=True, vmem_limit_bytes=VMEM_LIMIT),
    )(*(pltpu.with_memory_space_constraint(a, pltpu.HBM)
        for a in (source, fill, material, thickness, perm_table, stiff_table)))


def solution(mesh):
    return jax.shard_map(
        body,
        mesh=mesh,
        in_specs=(
            P("gx", "gy", "grp"),
            P("gx", "gy", "grp"),
            P("gx", "gy", "grp"),
            P("gx", "gy"),
            P(),
            P(),
        ),
        out_specs=(P("gx", "gy", "grp"), P("gx", "gy", "grp"), P("gx", "gy")),
        check_vma=False,
    )
```

```python
import jax
import jax.numpy as jnp
from jax import lax
from jax.experimental import pallas as pl
from jax.experimental.pallas import tpu as pltpu
from jax.sharding import PartitionSpec as P

W = 4
VMEM_LIMIT = 24 << 20
MESH = pl.DeviceIdType.MESH
DIRS = [(-1, -1), (-1, 0), (-1, 1), (0, -1), (0, 1), (1, -1), (1, 0), (1, 1)]
NINE = [(0, 0)] + DIRS
ORDER = [0, 1, 2, 3, 4, 5, 6, 7]
FACES = 2


def spread(table, material, count):
    total = jnp.zeros(material.shape, jnp.float32)
    for entry in range(count):
        total = jnp.where(material == entry, table[entry], total)
    return total


def make_kernel(nx, ny, nz, ngx, ngy, mats):
    rows, depth = ny // 2, 2 * nz
    ex, ey = nx + 2 * W, rows + 2 * W
    nslab = 2 * ngy
    levels = depth.bit_length() - 1

    def blocks(dx, dy, reach):
        xr = reach - abs(dy)
        yr = reach - abs(dx)
        xs, xd = {-1: ((0, xr), (W + nx, xr)), 0: ((0, nx), (W, nx)), 1: ((nx - xr, xr), (W - xr, xr))}[dx]
        ys, yd = {-1: ((0, yr), (rows, yr)), 0: ((0, rows), (0, rows)),
                  1: ((rows - yr, yr), (ey - yr, yr))}[dy]
        return xs, ys, xd, yd

    def blocks_for(dx, dy, reach):
        _, (ys, yn), _, (yd, _) = blocks(0, dy, reach)
        xr = reach - abs(dy)
        yn, ys, yd = (yn, ys, yd) if dy == 0 else (reach - 1, ys + (1 if dy == 1 else 0), yd + (1 if dy == 1 else 0))
        xs = jnp.where(dx == -1, 0, nx - xr)
        xd = jnp.where(dx == -1, W + nx, W - xr)
        return (xs, xr), (ys, yn), (xd, xr), (yd, yn)

    def kernel(source, fill, material, thickness, perm_table, stiff_table, p_out, d_out, th_out,
               s_ext, f_ext, k_ext, px0, px1, px2, ta, tb, gx_, gy_, gz_, a_,
               alpha, gamma, inv, wts, cols, fin_p, fin_d, mat, kloc, stloc, st, thick, line, line_in, perm, stiffs,
               csend, crecv, cloc, send, recv, psend, precv, loc):
        g = lax.axis_index("grp")
        ix = lax.axis_index("gx")
        iy = lax.axis_index("gy")
        slab = 2 * iy + g
        far = jnp.where(lax.rem(ix, 4) < 2, -1, 1)
        other = 1 - g

        def within(value, count):
            return jnp.where(value >= 0, 1, 0) * jnp.where(value < count, 1, 0)

        def place(dx, dy):
            x = jnp.clip(ix + dx, 0, ngx - 1)
            if dy == 0:
                return {"grp": g, "gx": x, "gy": iy}
            return {"grp": other, "gx": x, "gy": jnp.clip(iy + (g if dy == 1 else g - 1), 0, ngy - 1)}

        alive = [within(ix + dx, ngx) * within(slab + dy, nslab) for dx, dy in DIRS]

        barrier = pltpu.get_barrier_semaphore()
        for dx in (far, 0, -far):
            for dgy in (2 * g - 1, 0):
                for core in range(2):
                    ok = within(ix + dx, ngx) * within(iy + dgy, ngy)
                    if isinstance(dx, int) and isinstance(dgy, int):
                        ok = jnp.where(g == core, 0, 1)

                    @pl.when(ok == 1)
                    def _():
                        target = {"grp": core, "gx": jnp.clip(ix + dx, 0, ngx - 1),
                                  "gy": jnp.clip(iy + dgy, 0, ngy - 1)}
                        pl.semaphore_signal(barrier, 1, device_id=target, device_id_type=MESH)
        greeted = (sum(within(ix + dx, ngx) for dx in (-1, 0, 1))
                   * sum(within(2 * iy + j, nslab) for j in (-1, 0, 1, 2)) - 1)

        load_th = pltpu.make_async_copy(thickness, thick, loc.at[0])
        load_mat = pltpu.make_async_copy(material, mat, loc.at[1])
        load_perm = pltpu.make_async_copy(perm_table, perm, loc.at[6])
        load_stiff = pltpu.make_async_copy(stiff_table, stiffs, loc.at[7])
        for c in (load_th, load_mat, load_perm, load_stiff):
            c.start()

        for i in range(8):
            dx, dy = DIRS[i]
            _, _, (x0, xn), (y0, yn) = blocks(-dx, -dy, W)

            @pl.when(alive[i] == 0)
            def _():
                s_ext[x0:x0 + xn, y0:y0 + yn, :] = jnp.zeros((xn, yn, depth), jnp.float32)
                f_ext[x0:x0 + xn, y0:y0 + yn, :] = jnp.zeros((xn, yn, depth), jnp.int32)
                k_ext[x0:x0 + xn, y0:y0 + yn, :] = jnp.zeros((xn, yn, depth), jnp.float32)
                for ref in (px0, px1, px2):
                    ref[x0:x0 + xn, y0:y0 + yn, :] = jnp.zeros((xn, yn, depth), jnp.float32)
                cols[1 + dx, y0:y0 + yn, :] = jnp.zeros((yn, 128), jnp.float32)

        for c in (load_th, load_mat, load_perm, load_stiff):
            c.wait()
        diagonal = lax.broadcasted_iota(jnp.int32, (ny, ny), 0) == lax.broadcasted_iota(jnp.int32, (ny, ny), 1)
        for x in range(nx):
            across = jnp.broadcast_to(thick[x:x + 1, :], (ny, ny))
            t = jnp.sum(jnp.where(diagonal, across, 0.0), axis=1, keepdims=True)
            m = mat[x]
            kloc[x] = spread(perm, m, mats) * (t * t * t)
            stloc[x] = spread(stiffs, m, mats)

        pl.semaphore_wait(barrier, greeted)

        mine = pl.multiple_of(g * rows, rows)
        theirs = pl.multiple_of(other * rows, rows)
        z_here = pl.multiple_of(g * nz, nz)
        z_there = pl.multiple_of(other * nz, nz)
        consts = [(0, kloc, k_ext, W), (1, fill, f_ext, W - 1), (2, source, s_ext, W - 1)]

        def const_send(n, v, dx, dy, local=False):
            _, src, ext, reach = consts[n]
            if dx is None:
                (xs, xn), (ys, yn), (xd, _), (yd, _) = blocks(0, dy, reach)
                i, x = NINE.index((0, dy)), ix
            else:
                (xs, xn), (ys, yn), (xd, _), (yd, _) = blocks_for(dx, dy, reach)
                i, x = jnp.where(dx == -1, 2, 7) + dy, jnp.clip(ix + dx, 0, ngx - 1)
            core, dgy = (v + dy) % 2, (v + dy) // 2
            from_ = src.at[pl.ds(xs, xn), pl.ds(v * rows + ys, yn), :]
            to = ext.at[pl.ds(xd, xn), pl.ds(yd, yn), pl.ds(z_here, nz)]
            target = {"grp": core, "gx": x, "gy": jnp.clip(iy + dgy, 0, ngy - 1)}
            if local:
                return pltpu.make_async_copy(from_, to, cloc.at[n, 0 if dy == 0 else 1])
            return pltpu.make_async_remote_copy(
                from_, to, csend.at[n, v, i], crecv.at[n, g, i], device_id=target, device_id_type=MESH)

        def const_each(do_away, do_keep):
            for dx in (far, None, -far):
                for v in range(2):
                    for dy in (0, 1, -1):
                        core, dgy = (v + dy) % 2, (v + dy) // 2
                        if dx is None:
                            ok = within(iy + dgy, ngy)
                            if dgy == 0:
                                ok = jnp.where(g == core, 0, 1)
                                if do_keep is not None:
                                    @pl.when(g == core)
                                    def _():
                                        for n in range(3):
                                            do_keep(const_send(n, v, dx, dy, True))
                        else:
                            ok = within(ix + dx, ngx) * within(iy + dgy, ngy)

                        @pl.when(ok == 1)
                        def _():
                            for n in range(3):
                                do_away(const_send(n, v, dx, dy))

        def const_arrive(group):
            for src in range(2):
                for i in range(9):
                    dx, dy = NINE[i]
                    ok = within(ix - dx, ngx) * within(slab - dy, nslab)
                    if dx == 0:
                        here = jnp.where(g == src, 1, 0)
                        if dy == 1:
                            here = here * g
                        if dy == -1:
                            here = here * other
                        ok = ok * (1 - here)

                        @pl.when(here == 1)
                        def _():
                            for n in group:
                                _, ref, ext, reach = consts[n]
                                (xs, xn), (ys, yn), (xd, _), (yd, _) = blocks(dx, dy, reach)
                                pltpu.make_async_copy(
                                    ref.at[pl.ds(xs, xn), pl.ds(ys, yn), :],
                                    ext.at[pl.ds(xd, xn), pl.ds(yd, yn), pl.ds(src * nz, nz)],
                                    cloc.at[n, 0 if dy == 0 else 1]).wait()

                    @pl.when(ok == 1)
                    def _():
                        for n in group:
                            _, ref, ext, reach = consts[n]
                            (xs, xn), (ys, yn), (xd, _), (yd, _) = blocks(dx, dy, reach)
                            pltpu.make_async_remote_copy(
                                ref.at[pl.ds(xs, xn), pl.ds(ys, yn), :],
                                ext.at[pl.ds(xd, xn), pl.ds(yd, yn), pl.ds(src * nz, nz)],
                                csend.at[n, 0, i], crecv.at[n, src, i],
                                device_id={"grp": other}, device_id_type=MESH).wait_recv()

        st_away = pltpu.make_async_remote_copy(
            stloc.at[:, pl.ds(theirs, rows), :], st.at[:, :, pl.ds(z_here, nz)],
            psend.at[0], precv.at[0], device_id={"grp": other}, device_id_type=MESH)
        st_keep = pltpu.make_async_copy(
            stloc.at[:, pl.ds(mine, rows), :], st.at[:, :, pl.ds(z_here, nz)], loc.at[2])
        st_away.start()
        st_keep.start()
        const_each(lambda c: c.start(), lambda c: c.start())

        def hop(e, ref, i):
            dx, dy = DIRS[i]
            (xs, xn), (ys, yn), (xd, _), (yd, _) = blocks(dx, dy, W)
            if ref is cols:
                src = ref.at[1, pl.ds(ys, yn), :]
                dst = ref.at[1 - dx, pl.ds(yd, yn), :]
            else:
                src = ref.at[pl.ds(W + xs, xn), pl.ds(ys, yn), :]
                dst = ref.at[pl.ds(xd, xn), pl.ds(yd, yn), :]
            return pltpu.make_async_remote_copy(
                src, dst, send.at[e, i], recv.at[e, i], device_id=place(dx, dy), device_id_type=MESH)

        def push(e, ref):
            for dx in (far, None, -far):
                for dy in ((0, 1, -1) if dx is not None else (1, -1)):
                    if dx is None:
                        (xs, xn), (ys, yn), (xd, _), (yd, _) = blocks(0, dy, W)
                        i, x, into = DIRS.index((0, dy)), ix, 1
                    else:
                        (xs, xn), (ys, yn), (xd, _), (yd, _) = blocks_for(dx, dy, W)
                        i, x, into = jnp.where(dx == -1, 1, 6) + dy, jnp.clip(ix + dx, 0, ngx - 1), 1 - dx
                    if ref is cols:
                        src, dst = ref.at[1, pl.ds(ys, yn), :], ref.at[into, pl.ds(yd, yn), :]
                    else:
                        src = ref.at[pl.ds(W + xs, xn), pl.ds(ys, yn), :]
                        dst = ref.at[pl.ds(xd, xn), pl.ds(yd, yn), :]
                    target = place(0, dy)
                    target["gx"] = x
                    ok = within(x if dx is None else ix + dx, ngx) * within(slab + dy, nslab)

                    @pl.when(ok == 1)
                    def _():
                        pltpu.make_async_remote_copy(
                            src, dst, send.at[e, i], recv.at[e, i], device_id=target, device_id_type=MESH).start()

        def arrive(e, ref):
            for i in range(8):
                @pl.when(alive[7 - i] == 1)
                def _():
                    hop(e, ref, i).wait_recv()

        def sent(e, ref):
            for i in range(8):
                @pl.when(alive[i] == 1)
                def _():
                    hop(e, ref, i).wait_send()

        zpos = lax.broadcasted_iota(jnp.int32, (rows, depth), 1)

        def reduce_columns(x, carry):
            s = st[x] * (1.0 - 0.5 * f_ext[W + x, 0:rows, :].astype(jnp.float32))
            low = jnp.where(zpos == 0, 0.0, pltpu.roll(s, 1, 1))
            high = jnp.where(zpos == depth - 1, 0.0, pltpu.roll(s, depth - 1, 1))
            up = 0.5 * (s + high)
            down = 0.5 * (s + low)
            a = jnp.where(zpos == 0, 0.0, down)
            c = jnp.where(zpos == depth - 1, 0.0, up)
            e = 0.001 * s + jnp.where(zpos == 0, down, 0.0) + jnp.where(zpos == depth - 1, up, 0.0)
            r = jnp.full((rows, depth), 0.001 / depth, jnp.float32)
            for level in range(levels):
                stride = 1 << level
                back = depth - stride
                recip = 1.0 / (a + c + e)
                al = a * pltpu.roll(recip, stride, 1)
                ga = c * pltpu.roll(recip, back, 1)
                alpha[level, x] = al
                gamma[level, x] = ga
                a = al * pltpu.roll(a, stride, 1)
                c = ga * pltpu.roll(c, back, 1)
                e = e + al * pltpu.roll(e, stride, 1) + ga * pltpu.roll(e, back, 1)
                r = r + al * pltpu.roll(r, stride, 1) + ga * pltpu.roll(r, back, 1)
            recip = 1.0 / e
            inv[x] = recip
            wts[x] = r * recip
            return carry

        zfull = lax.broadcasted_iota(jnp.int32, (ey, depth), 1)

        def faces(x, carry):
            k = k_ext[x]
            front = jnp.where(zfull == 0, 0.0, pltpu.roll(k, 1, 1))
            back = jnp.where(zfull == depth - 1, 0.0, pltpu.roll(k, depth - 1, 1))
            gzp = 0.5 * (k + back)
            gzm = 0.5 * (k + front)
            gyp = 0.5 * (k + pltpu.roll(k, ey - 1, 0))
            gym = 0.5 * (k + pltpu.roll(k, 1, 0))
            gxp = 0.5 * (k + k_ext[x + 1])
            gxm = 0.5 * (k + k_ext[x - 1])
            fl = f_ext[x].astype(jnp.float32)
            denom = gxp + gxm + gyp + gym + gzp + gzm + 1.0 - fl
            gx_[x] = gxp
            gy_[x] = gyp
            gz_[x] = jnp.where(zfull == depth - 1, 0.0, gzp)
            a_[x] = fl / denom
            return carry

        def all_faces():
            gx_[0] = 0.5 * (k_ext[0] + k_ext[1])
            lax.fori_loop(1, ex - 1, faces, 0, unroll=FACES)

        def relax(src, dst, level, width):
            def one(x, carry):
                here = src[x]
                gy = gy_[x]
                gz = gz_[x]
                total = s_ext[x] + gx_[x] * src[x + 1] + gx_[x - 1] * src[x - 1]
                total = total + gy * pltpu.roll(here, ey - 1, 0) + pltpu.roll(gy * here, 1, 0)
                total = total + gz * pltpu.roll(here, depth - 1, 1) + pltpu.roll(gz * here, 1, 1)
                value = a_[x] * total
                if width == ey:
                    dst[x] = value
                elif dst is fin_p:
                    dst[x - W] = value[0:width]
                else:
                    dst[x, 0:width] = value[0:width]
                return carry

            lax.fori_loop(level, ex - level, one, 0, unroll=ex - 2 * level)

        def first(x, carry):
            ta[x] = a_[x] * s_ext[x]
            return carry

        lane = lax.broadcasted_iota(jnp.int32, (rows, 128), 1)

        def mean_factor(held, base):
            comp = jnp.zeros((rows, 128), jnp.float32)
            for x in range(nx):
                part = wts[x] * (1.0 - held[base + x, 0:rows, :])
                comp = jnp.where(lane == x, jnp.sum(part, axis=1, keepdims=True), comp)
            return 1.0 + 0.3 * jnp.tanh(comp)

        st_away.wait_recv()
        st_keep.wait()
        const_arrive((0, 1))
        all_faces()
        const_arrive((2,))
        lax.fori_loop(1, ex - 1, first, 0, unroll=2)
        relax(ta, tb, 2, ey)
        relax(tb, ta, 3, ey)
        relax(ta, px0, 4, rows)
        push(0, px0)
        lax.fori_loop(0, nx, reduce_columns, 0)
        const_each(lambda c: c.wait_send(), None)
        st_away.wait_send()
        arrive(0, px0)
        relax(px0, ta, 1, ey)
        relax(ta, tb, 2, ey)
        relax(tb, ta, 3, ey)
        relax(ta, px1, 4, rows)

        factor = mean_factor(px1, W)
        cols[1, 0:rows, :] = factor
        push(2, cols)
        push(1, px1)
        sent(0, px0)
        arrive(2, cols)
        for x in range(ex):
            part, pos = (0, x + nx - W) if x < W else ((1, x - W) if x < W + nx else (2, x - W - nx))
            t = cols[part, :, pos:pos + 1]
            k_ext[x] = k_ext[x] * (t * t * t)
        all_faces()
        arrive(1, px1)
        relax(px1, ta, 1, ey)
        relax(ta, tb, 2, ey)
        relax(tb, ta, 3, ey)
        relax(ta, px2, 4, rows)
        push(3, px2)
        sent(2, cols)
        sent(1, px1)
        arrive(3, px2)
        relax(px2, ta, 1, ey)
        relax(ta, tb, 2, ey)
        relax(tb, ta, 3, ey)
        relax(ta, fin_p, 4, rows)

        def give(n, ref, dst, x0, xn):
            out = pltpu.make_async_remote_copy(
                ref.at[pl.ds(x0, xn), :, pl.ds(z_there, nz)], dst.at[pl.ds(x0, xn), pl.ds(mine, rows), :],
                psend.at[n], precv.at[n], device_id={"grp": other}, device_id_type=MESH)
            keep = pltpu.make_async_copy(
                ref.at[pl.ds(x0, xn), :, pl.ds(z_here, nz)], dst.at[pl.ds(x0, xn), pl.ds(mine, rows), :],
                loc.at[2 + n])
            return out, keep

        half = nx // 2
        gives = [give(1, fin_p, p_out, 0, nx), give(2, fin_d, d_out, 0, half), give(3, fin_d, d_out, half, half)]
        for c in gives[0]:
            c.start()

        def solve_columns(x, carry):
            r = 0.001 * (1.0 - fin_p[x])
            for level in range(levels):
                stride = 1 << level
                r = (r + alpha[level, x] * pltpu.roll(r, stride, 1)
                     + gamma[level, x] * pltpu.roll(r, depth - stride, 1))
            fin_d[x] = r * inv[x]
            return carry

        for n in range(2):
            lax.fori_loop(n * half, (n + 1) * half, solve_columns, 0, unroll=half)
            for c in gives[1 + n]:
                c.start()

        factor = factor * mean_factor(fin_p, 0)
        spot = lane == lax.broadcasted_iota(jnp.int32, (rows, 128), 0) + g * rows
        pick = lax.broadcasted_iota(jnp.int32, (nx, 128), 0)
        mixed = jnp.zeros((nx, 128), jnp.float32)
        for x in range(nx):
            row = jnp.sum(jnp.where(spot, factor[:, x:x + 1], 0.0), axis=0, keepdims=True)
            mixed = jnp.where(pick == x, row, mixed)
        line[...] = mixed
        t_out = pltpu.make_async_remote_copy(
            line, line_in, psend.at[4], precv.at[4], device_id={"grp": other}, device_id_type=MESH)
        t_out.start()
        sent(3, px2)
        for out, keep in gives:
            out.wait_send()
            keep.wait()
        t_out.wait_send()
        t_out.wait_recv()
        th_out[...] = thick[...] * (mixed + line_in[...])[:, 0:ny]
        for out, keep in gives:
            out.wait_recv()

    return kernel, rows, depth, ex, ey, levels


def body(source, fill, material, thickness, perm_table, stiff_table):
    nx, ny, nz = source.shape
    kernel, rows, depth, ex, ey, levels = make_kernel(
        nx, ny, nz, lax.axis_size("gx"), lax.axis_size("gy"), perm_table.shape[0])
    f32, i32 = jnp.float32, jnp.int32
    vm = pl.BlockSpec(memory_space=pltpu.VMEM)
    hb = pl.BlockSpec(memory_space=pl.ANY)
    hbm = pl.BlockSpec(memory_space=pltpu.HBM)
    ext = pltpu.VMEM((ex, ey, depth), f32)
    iext = pltpu.VMEM((ex, ey, depth), i32)
    own = pltpu.VMEM((nx, rows, depth), f32)
    brick = pltpu.VMEM((nx, ny, nz), f32)
    dma = pltpu.SemaphoreType.DMA
    fields = pl.pallas_call(
        kernel,
        out_shape=(
            jax.ShapeDtypeStruct((nx, ny, nz), f32),
            jax.ShapeDtypeStruct((nx, ny, nz), f32),
            jax.ShapeDtypeStruct((nx, ny), f32),
        ),
        in_specs=[hbm] * 6,
        out_specs=(hb, hb, vm),
        scratch_shapes=[
            ext, iext, ext, ext, ext, ext, ext, ext, ext, ext, ext, ext,
            pltpu.VMEM((levels, nx, rows, depth), f32),
            pltpu.VMEM((levels, nx, rows, depth), f32),
            own, own,
            pltpu.VMEM((3, ey, 128), f32),
            own, own,
            pltpu.VMEM((nx, ny, nz), i32), brick, brick, own,
            pltpu.VMEM((nx, ny), f32),
            pltpu.VMEM((nx, 128), f32),
            pltpu.VMEM((nx, 128), f32),
            pltpu.SMEM(perm_table.shape, f32), pltpu.SMEM(stiff_table.shape, f32),
            dma((3, 2, 9)), dma((3, 2, 9)), dma((3, 2)),
            dma((4, 8)), dma((4, 8)), dma((5,)), dma((5,)), dma((8,)),
        ],
        compiler_params=pltpu.CompilerParams(
            collective_id=0, has_side_effects=True, vmem_limit_bytes=VMEM_LIMIT),
    )(*(pltpu.with_memory_space_constraint(a, pltpu.HBM)
        for a in (source, fill, material, thickness, perm_table, stiff_table)))

    def settle(*refs):
        ins, outs, sems = refs[:3], refs[3:6], refs[6]
        copies = [pltpu.make_async_copy(i, o, sems.at[n]) for n, (i, o) in enumerate(zip(ins, outs))]
        for c in copies:
            c.start()
        for c in copies:
            c.wait()

    return pl.pallas_call(
        settle,
        out_shape=tuple(jax.ShapeDtypeStruct(a.shape, f32) for a in fields),
        in_specs=[hb] * 3,
        out_specs=(hbm,) * 3,
        scratch_shapes=[dma((3,))],
        compiler_params=pltpu.CompilerParams(vmem_limit_bytes=1 << 20),
    )(*fields)


def solution(mesh):
    return jax.shard_map(
        body,
        mesh=mesh,
        in_specs=(
            P("gx", "gy", "grp"),
            P("gx", "gy", "grp"),
            P("gx", "gy", "grp"),
            P("gx", "gy"),
            P(),
            P(),
        ),
        out_specs=(P("gx", "gy", "grp"), P("gx", "gy", "grp"), P("gx", "gy")),
        check_vma=False,
    )
```

```python
import jax
import jax.numpy as jnp
from jax import lax
from jax.experimental import pallas as pl
from jax.experimental.pallas import tpu as pltpu
from jax.sharding import PartitionSpec as P

W = 4
VMEM_LIMIT = 24 << 20
MESH = pl.DeviceIdType.MESH
DIRS = [(-1, -1), (-1, 0), (-1, 1), (0, -1), (0, 1), (1, -1), (1, 0), (1, 1)]
NINE = [(0, 0)] + DIRS
ORDER = [0, 1, 2, 3, 4, 5, 6, 7]
FACES = 14


def spread(table, material, count):
    total = jnp.zeros(material.shape, jnp.float32)
    for entry in range(count):
        total = jnp.where(material == entry, table[entry], total)
    return total


def make_kernel(nx, ny, nz, ngx, ngy, mats):
    rows, depth = ny // 2, 2 * nz
    ex, ey = nx + 2 * W, rows + 2 * W
    nslab = 2 * ngy
    levels = depth.bit_length() - 1

    def blocks(dx, dy, reach):
        xr = reach - abs(dy)
        yr = reach - abs(dx)
        xs, xd = {-1: ((0, xr), (W + nx, xr)), 0: ((0, nx), (W, nx)), 1: ((nx - xr, xr), (W - xr, xr))}[dx]
        ys, yd = {-1: ((0, yr), (rows, yr)), 0: ((0, rows), (0, rows)),
                  1: ((rows - yr, yr), (ey - yr, yr))}[dy]
        return xs, ys, xd, yd

    def blocks_for(dx, dy, reach):
        _, (ys, yn), _, (yd, _) = blocks(0, dy, reach)
        xr = reach - abs(dy)
        yn, ys, yd = (yn, ys, yd) if dy == 0 else (reach - 1, ys + (1 if dy == 1 else 0), yd + (1 if dy == 1 else 0))
        xs = jnp.where(dx == -1, 0, nx - xr)
        xd = jnp.where(dx == -1, W + nx, W - xr)
        return (xs, xr), (ys, yn), (xd, xr), (yd, yn)

    def kernel(source, fill, material, thickness, perm_table, stiff_table, p_out, d_out, th_out,
               s_ext, f_ext, k_ext, px0, px1, px2, ta, tb, gx_, gy_, gz_, a_,
               alpha, gamma, inv, wts, cols, fin_p, fin_d, mat, kloc, stloc, st, thick, line, line_in, perm, stiffs,
               csend, crecv, cloc, send, recv, psend, precv, loc):
        g = lax.axis_index("grp")
        ix = lax.axis_index("gx")
        iy = lax.axis_index("gy")
        slab = 2 * iy + g
        far = jnp.where(lax.rem(ix, 4) < 2, -1, 1)
        other = 1 - g

        def within(value, count):
            return jnp.where(value >= 0, 1, 0) * jnp.where(value < count, 1, 0)

        def place(dx, dy):
            x = jnp.clip(ix + dx, 0, ngx - 1)
            if dy == 0:
                return {"grp": g, "gx": x, "gy": iy}
            return {"grp": other, "gx": x, "gy": jnp.clip(iy + (g if dy == 1 else g - 1), 0, ngy - 1)}

        alive = [within(ix + dx, ngx) * within(slab + dy, nslab) for dx, dy in DIRS]

        barrier = pltpu.get_barrier_semaphore()
        for dx in (far, 0, -far):
            for dgy in (2 * g - 1, 0):
                for core in range(2):
                    ok = within(ix + dx, ngx) * within(iy + dgy, ngy)
                    if isinstance(dx, int) and isinstance(dgy, int):
                        ok = jnp.where(g == core, 0, 1)

                    @pl.when(ok == 1)
                    def _():
                        target = {"grp": core, "gx": jnp.clip(ix + dx, 0, ngx - 1),
                                  "gy": jnp.clip(iy + dgy, 0, ngy - 1)}
                        pl.semaphore_signal(barrier, 1, device_id=target, device_id_type=MESH)
        greeted = (sum(within(ix + dx, ngx) for dx in (-1, 0, 1))
                   * sum(within(2 * iy + j, nslab) for j in (-1, 0, 1, 2)) - 1)

        load_th = pltpu.make_async_copy(thickness, thick, loc.at[0])
        load_mat = pltpu.make_async_copy(material, mat, loc.at[1])
        load_perm = pltpu.make_async_copy(perm_table, perm, loc.at[6])
        load_stiff = pltpu.make_async_copy(stiff_table, stiffs, loc.at[7])
        for c in (load_th, load_mat, load_perm, load_stiff):
            c.start()

        for i in range(8):
            dx, dy = DIRS[i]
            _, _, (x0, xn), (y0, yn) = blocks(-dx, -dy, W)

            @pl.when(alive[i] == 0)
            def _():
                s_ext[x0:x0 + xn, y0:y0 + yn, :] = jnp.zeros((xn, yn, depth), jnp.float32)
                f_ext[x0:x0 + xn, y0:y0 + yn, :] = jnp.zeros((xn, yn, depth), jnp.int32)
                k_ext[x0:x0 + xn, y0:y0 + yn, :] = jnp.zeros((xn, yn, depth), jnp.float32)
                for ref in (px0, px1, px2):
                    ref[x0:x0 + xn, y0:y0 + yn, :] = jnp.zeros((xn, yn, depth), jnp.float32)
                cols[1 + dx, y0:y0 + yn, :] = jnp.zeros((yn, 128), jnp.float32)

        for c in (load_th, load_mat, load_perm, load_stiff):
            c.wait()
        diagonal = lax.broadcasted_iota(jnp.int32, (ny, ny), 0) == lax.broadcasted_iota(jnp.int32, (ny, ny), 1)
        for x in range(nx):
            across = jnp.broadcast_to(thick[x:x + 1, :], (ny, ny))
            t = jnp.sum(jnp.where(diagonal, across, 0.0), axis=1, keepdims=True)
            m = mat[x]
            kloc[x] = spread(perm, m, mats) * (t * t * t)
            stloc[x] = spread(stiffs, m, mats)

        pl.semaphore_wait(barrier, greeted)

        mine = pl.multiple_of(g * rows, rows)
        theirs = pl.multiple_of(other * rows, rows)
        z_here = pl.multiple_of(g * nz, nz)
        z_there = pl.multiple_of(other * nz, nz)
        consts = [(0, kloc, k_ext, W), (1, fill, f_ext, W - 1), (2, source, s_ext, W - 1)]

        def const_send(n, v, dx, dy, local=False):
            _, src, ext, reach = consts[n]
            if dx is None:
                (xs, xn), (ys, yn), (xd, _), (yd, _) = blocks(0, dy, reach)
                i, x = NINE.index((0, dy)), ix
            else:
                (xs, xn), (ys, yn), (xd, _), (yd, _) = blocks_for(dx, dy, reach)
                i, x = jnp.where(dx == -1, 2, 7) + dy, jnp.clip(ix + dx, 0, ngx - 1)
            core, dgy = (v + dy) % 2, (v + dy) // 2
            from_ = src.at[pl.ds(xs, xn), pl.ds(v * rows + ys, yn), :]
            to = ext.at[pl.ds(xd, xn), pl.ds(yd, yn), pl.ds(z_here, nz)]
            target = {"grp": core, "gx": x, "gy": jnp.clip(iy + dgy, 0, ngy - 1)}
            if local:
                return pltpu.make_async_copy(from_, to, cloc.at[n, 0 if dy == 0 else 1])
            return pltpu.make_async_remote_copy(
                from_, to, csend.at[n, v, i], crecv.at[n, g, i], device_id=target, device_id_type=MESH)

        def const_each(do_away, do_keep):
            for dx in (far, None, -far):
                for v in range(2):
                    for dy in (0, 1, -1):
                        core, dgy = (v + dy) % 2, (v + dy) // 2
                        if dx is None:
                            ok = within(iy + dgy, ngy)
                            if dgy == 0:
                                ok = jnp.where(g == core, 0, 1)
                                if do_keep is not None:
                                    @pl.when(g == core)
                                    def _():
                                        for n in range(3):
                                            do_keep(const_send(n, v, dx, dy, True))
                        else:
                            ok = within(ix + dx, ngx) * within(iy + dgy, ngy)

                        @pl.when(ok == 1)
                        def _():
                            for n in range(3):
                                do_away(const_send(n, v, dx, dy))

        def const_arrive(group):
            for src in range(2):
                for i in range(9):
                    dx, dy = NINE[i]
                    ok = within(ix - dx, ngx) * within(slab - dy, nslab)
                    if dx == 0:
                        here = jnp.where(g == src, 1, 0)
                        if dy == 1:
                            here = here * g
                        if dy == -1:
                            here = here * other
                        ok = ok * (1 - here)

                        @pl.when(here == 1)
                        def _():
                            for n in group:
                                _, ref, ext, reach = consts[n]
                                (xs, xn), (ys, yn), (xd, _), (yd, _) = blocks(dx, dy, reach)
                                pltpu.make_async_copy(
                                    ref.at[pl.ds(xs, xn), pl.ds(ys, yn), :],
                                    ext.at[pl.ds(xd, xn), pl.ds(yd, yn), pl.ds(src * nz, nz)],
                                    cloc.at[n, 0 if dy == 0 else 1]).wait()

                    @pl.when(ok == 1)
                    def _():
                        for n in group:
                            _, ref, ext, reach = consts[n]
                            (xs, xn), (ys, yn), (xd, _), (yd, _) = blocks(dx, dy, reach)
                            pltpu.make_async_remote_copy(
                                ref.at[pl.ds(xs, xn), pl.ds(ys, yn), :],
                                ext.at[pl.ds(xd, xn), pl.ds(yd, yn), pl.ds(src * nz, nz)],
                                csend.at[n, 0, i], crecv.at[n, src, i],
                                device_id={"grp": other}, device_id_type=MESH).wait_recv()

        st_away = pltpu.make_async_remote_copy(
            stloc.at[:, pl.ds(theirs, rows), :], st.at[:, :, pl.ds(z_here, nz)],
            psend.at[0], precv.at[0], device_id={"grp": other}, device_id_type=MESH)
        st_keep = pltpu.make_async_copy(
            stloc.at[:, pl.ds(mine, rows), :], st.at[:, :, pl.ds(z_here, nz)], loc.at[2])
        st_away.start()
        st_keep.start()
        const_each(lambda c: c.start(), lambda c: c.start())

        def hop(e, ref, i):
            dx, dy = DIRS[i]
            (xs, xn), (ys, yn), (xd, _), (yd, _) = blocks(dx, dy, W)
            if ref is cols:
                src = ref.at[1, pl.ds(ys, yn), :]
                dst = ref.at[1 - dx, pl.ds(yd, yn), :]
            else:
                src = ref.at[pl.ds(W + xs, xn), pl.ds(ys, yn), :]
                dst = ref.at[pl.ds(xd, xn), pl.ds(yd, yn), :]
            return pltpu.make_async_remote_copy(
                src, dst, send.at[e, i], recv.at[e, i], device_id=place(dx, dy), device_id_type=MESH)

        def push(e, ref):
            for dx in (None, far, -far):
                for dy in ((0, 1, -1) if dx is not None else (1, -1)):
                    if dx is None:
                        (xs, xn), (ys, yn), (xd, _), (yd, _) = blocks(0, dy, W)
                        i, x, into = DIRS.index((0, dy)), ix, 1
                    else:
                        (xs, xn), (ys, yn), (xd, _), (yd, _) = blocks_for(dx, dy, W)
                        i, x, into = jnp.where(dx == -1, 1, 6) + dy, jnp.clip(ix + dx, 0, ngx - 1), 1 - dx
                    if ref is cols:
                        src, dst = ref.at[1, pl.ds(ys, yn), :], ref.at[into, pl.ds(yd, yn), :]
                    else:
                        src = ref.at[pl.ds(W + xs, xn), pl.ds(ys, yn), :]
                        dst = ref.at[pl.ds(xd, xn), pl.ds(yd, yn), :]
                    target = place(0, dy)
                    target["gx"] = x
                    ok = within(x if dx is None else ix + dx, ngx) * within(slab + dy, nslab)

                    @pl.when(ok == 1)
                    def _():
                        pltpu.make_async_remote_copy(
                            src, dst, send.at[e, i], recv.at[e, i], device_id=target, device_id_type=MESH).start()

        def arrive(e, ref):
            for i in range(8):
                @pl.when(alive[7 - i] == 1)
                def _():
                    hop(e, ref, i).wait_recv()

        def sent(e, ref):
            for i in range(8):
                @pl.when(alive[i] == 1)
                def _():
                    hop(e, ref, i).wait_send()

        zpos = lax.broadcasted_iota(jnp.int32, (rows, depth), 1)

        def reduce_columns(x, carry):
            s = st[x] * (1.0 - 0.5 * f_ext[W + x, 0:rows, :].astype(jnp.float32))
            low = jnp.where(zpos == 0, 0.0, pltpu.roll(s, 1, 1))
            high = jnp.where(zpos == depth - 1, 0.0, pltpu.roll(s, depth - 1, 1))
            up = 0.5 * (s + high)
            down = 0.5 * (s + low)
            a = jnp.where(zpos == 0, 0.0, down)
            c = jnp.where(zpos == depth - 1, 0.0, up)
            e = 0.001 * s + jnp.where(zpos == 0, down, 0.0) + jnp.where(zpos == depth - 1, up, 0.0)
            r = jnp.full((rows, depth), 0.001 / depth, jnp.float32)
            for level in range(levels):
                stride = 1 << level
                back = depth - stride
                recip = 1.0 / (a + c + e)
                al = a * pltpu.roll(recip, stride, 1)
                ga = c * pltpu.roll(recip, back, 1)
                alpha[level, x] = al
                gamma[level, x] = ga
                a = al * pltpu.roll(a, stride, 1)
                c = ga * pltpu.roll(c, back, 1)
                e = e + al * pltpu.roll(e, stride, 1) + ga * pltpu.roll(e, back, 1)
                r = r + al * pltpu.roll(r, stride, 1) + ga * pltpu.roll(r, back, 1)
            recip = 1.0 / e
            inv[x] = recip
            wts[x] = r * recip
            return carry

        zfull = lax.broadcasted_iota(jnp.int32, (ey, depth), 1)

        def faces(x, carry):
            k = k_ext[x]
            front = jnp.where(zfull == 0, 0.0, pltpu.roll(k, 1, 1))
            back = jnp.where(zfull == depth - 1, 0.0, pltpu.roll(k, depth - 1, 1))
            gzp = 0.5 * (k + back)
            gzm = 0.5 * (k + front)
            gyp = 0.5 * (k + pltpu.roll(k, ey - 1, 0))
            gym = 0.5 * (k + pltpu.roll(k, 1, 0))
            gxp = 0.5 * (k + k_ext[x + 1])
            gxm = 0.5 * (k + k_ext[x - 1])
            fl = f_ext[x].astype(jnp.float32)
            denom = gxp + gxm + gyp + gym + gzp + gzm + 1.0 - fl
            gx_[x] = gxp
            gy_[x] = gyp
            gz_[x] = jnp.where(zfull == depth - 1, 0.0, gzp)
            a_[x] = fl / denom
            return carry

        def all_faces():
            gx_[0] = 0.5 * (k_ext[0] + k_ext[1])
            lax.fori_loop(1, ex - 1, faces, 0, unroll=FACES)

        def relax(src, dst, level, width):
            def one(x, carry):
                here = src[x]
                gy = gy_[x]
                gz = gz_[x]
                total = s_ext[x] + gx_[x] * src[x + 1] + gx_[x - 1] * src[x - 1]
                total = total + gy * pltpu.roll(here, ey - 1, 0) + pltpu.roll(gy * here, 1, 0)
                total = total + gz * pltpu.roll(here, depth - 1, 1) + pltpu.roll(gz * here, 1, 1)
                value = a_[x] * total
                if width == ey:
                    dst[x] = value
                elif dst is fin_p:
                    dst[x - W] = value[0:width]
                else:
                    dst[x, 0:width] = value[0:width]
                return carry

            lax.fori_loop(level, ex - level, one, 0, unroll=ex - 2 * level)

        def first(x, carry):
            ta[x] = a_[x] * s_ext[x]
            return carry

        lane = lax.broadcasted_iota(jnp.int32, (rows, 128), 1)

        def mean_factor(held, base):
            comp = jnp.zeros((rows, 128), jnp.float32)
            for x in range(nx):
                part = wts[x] * (1.0 - held[base + x, 0:rows, :])
                comp = jnp.where(lane == x, jnp.sum(part, axis=1, keepdims=True), comp)
            return 1.0 + 0.3 * jnp.tanh(comp)

        st_away.wait_recv()
        st_keep.wait()
        const_arrive((0, 1))
        all_faces()
        const_arrive((2,))
        lax.fori_loop(1, ex - 1, first, 0, unroll=2)
        relax(ta, tb, 2, ey)
        relax(tb, ta, 3, ey)
        relax(ta, px0, 4, rows)
        push(0, px0)
        lax.fori_loop(0, nx, reduce_columns, 0)
        const_each(lambda c: c.wait_send(), None)
        st_away.wait_send()
        arrive(0, px0)
        relax(px0, ta, 1, ey)
        relax(ta, tb, 2, ey)
        relax(tb, ta, 3, ey)
        relax(ta, px1, 4, rows)

        factor = mean_factor(px1, W)
        cols[1, 0:rows, :] = factor
        push(2, cols)
        push(1, px1)
        sent(0, px0)
        arrive(2, cols)
        for x in range(ex):
            part, pos = (0, x + nx - W) if x < W else ((1, x - W) if x < W + nx else (2, x - W - nx))
            t = cols[part, :, pos:pos + 1]
            k_ext[x] = k_ext[x] * (t * t * t)
        all_faces()
        arrive(1, px1)
        relax(px1, ta, 1, ey)
        relax(ta, tb, 2, ey)
        relax(tb, ta, 3, ey)
        relax(ta, px2, 4, rows)
        push(3, px2)
        sent(2, cols)
        sent(1, px1)
        arrive(3, px2)
        relax(px2, ta, 1, ey)
        relax(ta, tb, 2, ey)
        relax(tb, ta, 3, ey)
        relax(ta, fin_p, 4, rows)

        def give(n, ref, dst, x0, xn):
            out = pltpu.make_async_remote_copy(
                ref.at[pl.ds(x0, xn), :, pl.ds(z_there, nz)], dst.at[pl.ds(x0, xn), pl.ds(mine, rows), :],
                psend.at[n], precv.at[n], device_id={"grp": other}, device_id_type=MESH)
            keep = pltpu.make_async_copy(
                ref.at[pl.ds(x0, xn), :, pl.ds(z_here, nz)], dst.at[pl.ds(x0, xn), pl.ds(mine, rows), :],
                loc.at[2 + n])
            return out, keep

        half = nx // 2
        gives = [give(1, fin_p, p_out, 0, nx), give(2, fin_d, d_out, 0, half), give(3, fin_d, d_out, half, half)]
        for c in gives[0]:
            c.start()

        def solve_columns(x, carry):
            r = 0.001 * (1.0 - fin_p[x])
            for level in range(levels):
                stride = 1 << level
                r = (r + alpha[level, x] * pltpu.roll(r, stride, 1)
                     + gamma[level, x] * pltpu.roll(r, depth - stride, 1))
            fin_d[x] = r * inv[x]
            return carry

        lax.fori_loop(0, nx, solve_columns, 0, unroll=nx)
        for n in range(2):
            for c in gives[1 + n]:
                c.start()

        factor = factor * mean_factor(fin_p, 0)
        spot = lane == lax.broadcasted_iota(jnp.int32, (rows, 128), 0) + g * rows
        pick = lax.broadcasted_iota(jnp.int32, (nx, 128), 0)
        mixed = jnp.zeros((nx, 128), jnp.float32)
        for x in range(nx):
            row = jnp.sum(jnp.where(spot, factor[:, x:x + 1], 0.0), axis=0, keepdims=True)
            mixed = jnp.where(pick == x, row, mixed)
        line[...] = mixed
        t_out = pltpu.make_async_remote_copy(
            line, line_in, psend.at[4], precv.at[4], device_id={"grp": other}, device_id_type=MESH)
        t_out.start()
        sent(3, px2)
        for out, keep in gives:
            out.wait_send()
            keep.wait()
        t_out.wait_send()
        t_out.wait_recv()
        th_out[...] = thick[...] * (mixed + line_in[...])[:, 0:ny]
        for out, keep in gives:
            out.wait_recv()

    return kernel, rows, depth, ex, ey, levels


def body(source, fill, material, thickness, perm_table, stiff_table):
    nx, ny, nz = source.shape
    kernel, rows, depth, ex, ey, levels = make_kernel(
        nx, ny, nz, lax.axis_size("gx"), lax.axis_size("gy"), perm_table.shape[0])
    f32, i32 = jnp.float32, jnp.int32
    vm = pl.BlockSpec(memory_space=pltpu.VMEM)
    hb = pl.BlockSpec(memory_space=pl.ANY)
    hbm = pl.BlockSpec(memory_space=pltpu.HBM)
    ext = pltpu.VMEM((ex, ey, depth), f32)
    iext = pltpu.VMEM((ex, ey, depth), i32)
    own = pltpu.VMEM((nx, rows, depth), f32)
    brick = pltpu.VMEM((nx, ny, nz), f32)
    dma = pltpu.SemaphoreType.DMA
    fields = pl.pallas_call(
        kernel,
        out_shape=(
            jax.ShapeDtypeStruct((nx, ny, nz), f32),
            jax.ShapeDtypeStruct((nx, ny, nz), f32),
            jax.ShapeDtypeStruct((nx, ny), f32),
        ),
        in_specs=[hbm] * 6,
        out_specs=(hb, hb, vm),
        scratch_shapes=[
            ext, iext, ext, ext, ext, ext, ext, ext, ext, ext, ext, ext,
            pltpu.VMEM((levels, nx, rows, depth), f32),
            pltpu.VMEM((levels, nx, rows, depth), f32),
            own, own,
            pltpu.VMEM((3, ey, 128), f32),
            own, own,
            pltpu.VMEM((nx, ny, nz), i32), brick, brick, own,
            pltpu.VMEM((nx, ny), f32),
            pltpu.VMEM((nx, 128), f32),
            pltpu.VMEM((nx, 128), f32),
            pltpu.SMEM(perm_table.shape, f32), pltpu.SMEM(stiff_table.shape, f32),
            dma((3, 2, 9)), dma((3, 2, 9)), dma((3, 2)),
            dma((4, 8)), dma((4, 8)), dma((5,)), dma((5,)), dma((8,)),
        ],
        compiler_params=pltpu.CompilerParams(
            collective_id=0, has_side_effects=True, vmem_limit_bytes=VMEM_LIMIT),
    )(*(pltpu.with_memory_space_constraint(a, pltpu.HBM)
        for a in (source, fill, material, thickness, perm_table, stiff_table)))

    def settle(*refs):
        ins, outs, sems = refs[:3], refs[3:6], refs[6]
        copies = [pltpu.make_async_copy(i, o, sems.at[n]) for n, (i, o) in enumerate(zip(ins, outs))]
        for c in copies:
            c.start()
        for c in copies:
            c.wait()

    return pl.pallas_call(
        settle,
        out_shape=tuple(jax.ShapeDtypeStruct(a.shape, f32) for a in fields),
        in_specs=[hb] * 3,
        out_specs=(hbm,) * 3,
        scratch_shapes=[dma((3,))],
        compiler_params=pltpu.CompilerParams(vmem_limit_bytes=1 << 20),
    )(*fields)


def solution(mesh):
    return jax.shard_map(
        body,
        mesh=mesh,
        in_specs=(
            P("gx", "gy", "grp"),
            P("gx", "gy", "grp"),
            P("gx", "gy", "grp"),
            P("gx", "gy"),
            P(),
            P(),
        ),
        out_specs=(P("gx", "gy", "grp"), P("gx", "gy", "grp"), P("gx", "gy")),
        check_vma=False,
    )
```

```python
import jax
import jax.numpy as jnp
from jax import lax
from jax.experimental import pallas as pl
from jax.experimental.pallas import tpu as pltpu
from jax.sharding import PartitionSpec as P

W = 4
VMEM_LIMIT = 24 << 20
MESH = pl.DeviceIdType.MESH
DIRS = [(-1, -1), (-1, 0), (-1, 1), (0, -1), (0, 1), (1, -1), (1, 0), (1, 1)]
NINE = [(0, 0)] + DIRS
ORDER = [0, 1, 2, 3, 4, 5, 6, 7]
FACES = 14


def spread(table, material, count):
    total = jnp.zeros(material.shape, jnp.float32)
    for entry in range(count):
        total = jnp.where(material == entry, table[entry], total)
    return total


def make_kernel(nx, ny, nz, ngx, ngy, mats):
    rows, depth = ny // 2, 2 * nz
    ex, ey = nx + 2 * W, rows + 2 * W
    nslab = 2 * ngy
    levels = depth.bit_length() - 1

    def blocks(dx, dy, reach):
        xr = reach - abs(dy)
        yr = reach - abs(dx)
        xs, xd = {-1: ((0, xr), (W + nx, xr)), 0: ((0, nx), (W, nx)), 1: ((nx - xr, xr), (W - xr, xr))}[dx]
        ys, yd = {-1: ((0, yr), (rows, yr)), 0: ((0, rows), (0, rows)),
                  1: ((rows - yr, yr), (ey - yr, yr))}[dy]
        return xs, ys, xd, yd

    def blocks_for(dx, dy, reach):
        _, (ys, yn), _, (yd, _) = blocks(0, dy, reach)
        xr = reach - abs(dy)
        yn, ys, yd = (yn, ys, yd) if dy == 0 else (reach - 1, ys + (1 if dy == 1 else 0), yd + (1 if dy == 1 else 0))
        xs = jnp.where(dx == -1, 0, nx - xr)
        xd = jnp.where(dx == -1, W + nx, W - xr)
        return (xs, xr), (ys, yn), (xd, xr), (yd, yn)

    def kernel(source, fill, material, thickness, perm_table, stiff_table, p_out, d_out, th_out,
               s_ext, f_ext, k_ext, px0, px1, px2, ta, tb, gx_, gy_, gz_, a_,
               alpha, gamma, inv, wts, cols, fin_p, fin_d, mat, kloc, stloc, st, thick, line, line_in, perm, stiffs,
               csend, crecv, cloc, send, recv, psend, precv, loc):
        g = lax.axis_index("grp")
        ix = lax.axis_index("gx")
        iy = lax.axis_index("gy")
        slab = 2 * iy + g
        far = jnp.where(lax.rem(ix, 4) < 2, -1, 1)
        other = 1 - g

        def within(value, count):
            return jnp.where(value >= 0, 1, 0) * jnp.where(value < count, 1, 0)

        def place(dx, dy):
            x = jnp.clip(ix + dx, 0, ngx - 1)
            if dy == 0:
                return {"grp": g, "gx": x, "gy": iy}
            return {"grp": other, "gx": x, "gy": jnp.clip(iy + (g if dy == 1 else g - 1), 0, ngy - 1)}

        alive = [within(ix + dx, ngx) * within(slab + dy, nslab) for dx, dy in DIRS]

        barrier = pltpu.get_barrier_semaphore()
        for dx in (far, 0, -far):
            for dgy in (2 * g - 1, 0):
                for core in range(2):
                    ok = within(ix + dx, ngx) * within(iy + dgy, ngy)
                    if isinstance(dx, int) and isinstance(dgy, int):
                        ok = jnp.where(g == core, 0, 1)

                    @pl.when(ok == 1)
                    def _():
                        target = {"grp": core, "gx": jnp.clip(ix + dx, 0, ngx - 1),
                                  "gy": jnp.clip(iy + dgy, 0, ngy - 1)}
                        pl.semaphore_signal(barrier, 1, device_id=target, device_id_type=MESH)
        greeted = (sum(within(ix + dx, ngx) for dx in (-1, 0, 1))
                   * sum(within(2 * iy + j, nslab) for j in (-1, 0, 1, 2)) - 1)

        load_th = pltpu.make_async_copy(thickness, thick, loc.at[0])
        load_mat = pltpu.make_async_copy(material, mat, loc.at[1])
        load_perm = pltpu.make_async_copy(perm_table, perm, loc.at[6])
        load_stiff = pltpu.make_async_copy(stiff_table, stiffs, loc.at[7])
        for c in (load_th, load_mat, load_perm, load_stiff):
            c.start()

        for i in range(8):
            dx, dy = DIRS[i]
            _, _, (x0, xn), (y0, yn) = blocks(-dx, -dy, W)

            @pl.when(alive[i] == 0)
            def _():
                s_ext[x0:x0 + xn, y0:y0 + yn, :] = jnp.zeros((xn, yn, depth), jnp.float32)
                f_ext[x0:x0 + xn, y0:y0 + yn, :] = jnp.zeros((xn, yn, depth), jnp.int32)
                k_ext[x0:x0 + xn, y0:y0 + yn, :] = jnp.zeros((xn, yn, depth), jnp.float32)
                for ref in (px0, px1, px2):
                    ref[x0:x0 + xn, y0:y0 + yn, :] = jnp.zeros((xn, yn, depth), jnp.float32)
                cols[1 + dx, y0:y0 + yn, :] = jnp.zeros((yn, 128), jnp.float32)

        for c in (load_th, load_mat, load_perm, load_stiff):
            c.wait()
        diagonal = lax.broadcasted_iota(jnp.int32, (ny, ny), 0) == lax.broadcasted_iota(jnp.int32, (ny, ny), 1)
        for x in range(nx):
            across = jnp.broadcast_to(thick[x:x + 1, :], (ny, ny))
            t = jnp.sum(jnp.where(diagonal, across, 0.0), axis=1, keepdims=True)
            m = mat[x]
            kloc[x] = spread(perm, m, mats) * (t * t * t)
            stloc[x] = spread(stiffs, m, mats)

        pl.semaphore_wait(barrier, greeted)

        mine = pl.multiple_of(g * rows, rows)
        theirs = pl.multiple_of(other * rows, rows)
        z_here = pl.multiple_of(g * nz, nz)
        z_there = pl.multiple_of(other * nz, nz)
        consts = [(0, kloc, k_ext, W), (1, fill, f_ext, W - 1), (2, source, s_ext, W - 1)]

        def const_send(n, v, dx, dy, local=False):
            _, src, ext, reach = consts[n]
            if dx is None:
                (xs, xn), (ys, yn), (xd, _), (yd, _) = blocks(0, dy, reach)
                i, x = NINE.index((0, dy)), ix
            else:
                (xs, xn), (ys, yn), (xd, _), (yd, _) = blocks_for(dx, dy, reach)
                i, x = jnp.where(dx == -1, 2, 7) + dy, jnp.clip(ix + dx, 0, ngx - 1)
            core, dgy = (v + dy) % 2, (v + dy) // 2
            from_ = src.at[pl.ds(xs, xn), pl.ds(v * rows + ys, yn), :]
            to = ext.at[pl.ds(xd, xn), pl.ds(yd, yn), pl.ds(z_here, nz)]
            target = {"grp": core, "gx": x, "gy": jnp.clip(iy + dgy, 0, ngy - 1)}
            if local:
                return pltpu.make_async_copy(from_, to, cloc.at[n, 0 if dy == 0 else 1])
            return pltpu.make_async_remote_copy(
                from_, to, csend.at[n, v, i], crecv.at[n, g, i], device_id=target, device_id_type=MESH)

        def const_each(do_away, do_keep):
            for dx in (far, None, -far):
                for v in range(2):
                    for dy in (0, 1, -1):
                        core, dgy = (v + dy) % 2, (v + dy) // 2
                        if dx is None:
                            ok = within(iy + dgy, ngy)
                            if dgy == 0:
                                ok = jnp.where(g == core, 0, 1)
                                if do_keep is not None:
                                    @pl.when(g == core)
                                    def _():
                                        for n in range(3):
                                            do_keep(const_send(n, v, dx, dy, True))
                        else:
                            ok = within(ix + dx, ngx) * within(iy + dgy, ngy)

                        @pl.when(ok == 1)
                        def _():
                            for n in range(3):
                                do_away(const_send(n, v, dx, dy))

        def const_arrive(group):
            for src in range(2):
                for i in range(9):
                    dx, dy = NINE[i]
                    ok = within(ix - dx, ngx) * within(slab - dy, nslab)
                    if dx == 0:
                        here = jnp.where(g == src, 1, 0)
                        if dy == 1:
                            here = here * g
                        if dy == -1:
                            here = here * other
                        ok = ok * (1 - here)

                        @pl.when(here == 1)
                        def _():
                            for n in group:
                                _, ref, ext, reach = consts[n]
                                (xs, xn), (ys, yn), (xd, _), (yd, _) = blocks(dx, dy, reach)
                                pltpu.make_async_copy(
                                    ref.at[pl.ds(xs, xn), pl.ds(ys, yn), :],
                                    ext.at[pl.ds(xd, xn), pl.ds(yd, yn), pl.ds(src * nz, nz)],
                                    cloc.at[n, 0 if dy == 0 else 1]).wait()

                    @pl.when(ok == 1)
                    def _():
                        for n in group:
                            _, ref, ext, reach = consts[n]
                            (xs, xn), (ys, yn), (xd, _), (yd, _) = blocks(dx, dy, reach)
                            pltpu.make_async_remote_copy(
                                ref.at[pl.ds(xs, xn), pl.ds(ys, yn), :],
                                ext.at[pl.ds(xd, xn), pl.ds(yd, yn), pl.ds(src * nz, nz)],
                                csend.at[n, 0, i], crecv.at[n, src, i],
                                device_id={"grp": other}, device_id_type=MESH).wait_recv()

        st_away = pltpu.make_async_remote_copy(
            stloc.at[:, pl.ds(theirs, rows), :], st.at[:, :, pl.ds(z_here, nz)],
            psend.at[0], precv.at[0], device_id={"grp": other}, device_id_type=MESH)
        st_keep = pltpu.make_async_copy(
            stloc.at[:, pl.ds(mine, rows), :], st.at[:, :, pl.ds(z_here, nz)], loc.at[2])
        st_away.start()
        st_keep.start()
        const_each(lambda c: c.start(), lambda c: c.start())

        def hop(e, ref, i):
            dx, dy = DIRS[i]
            (xs, xn), (ys, yn), (xd, _), (yd, _) = blocks(dx, dy, W)
            if ref is cols:
                src = ref.at[1, pl.ds(ys, yn), :]
                dst = ref.at[1 - dx, pl.ds(yd, yn), :]
            else:
                src = ref.at[pl.ds(W + xs, xn), pl.ds(ys, yn), :]
                dst = ref.at[pl.ds(xd, xn), pl.ds(yd, yn), :]
            return pltpu.make_async_remote_copy(
                src, dst, send.at[e, i], recv.at[e, i], device_id=place(dx, dy), device_id_type=MESH)

        def push(e, ref):
            for dx in (None, far, -far):
                for dy in ((0, 1, -1) if dx is not None else (1, -1)):
                    if dx is None:
                        (xs, xn), (ys, yn), (xd, _), (yd, _) = blocks(0, dy, W)
                        i, x, into = DIRS.index((0, dy)), ix, 1
                    else:
                        (xs, xn), (ys, yn), (xd, _), (yd, _) = blocks_for(dx, dy, W)
                        i, x, into = jnp.where(dx == -1, 1, 6) + dy, jnp.clip(ix + dx, 0, ngx - 1), 1 - dx
                    if ref is cols:
                        src, dst = ref.at[1, pl.ds(ys, yn), :], ref.at[into, pl.ds(yd, yn), :]
                    else:
                        src = ref.at[pl.ds(W + xs, xn), pl.ds(ys, yn), :]
                        dst = ref.at[pl.ds(xd, xn), pl.ds(yd, yn), :]
                    target = place(0, dy)
                    target["gx"] = x
                    ok = within(x if dx is None else ix + dx, ngx) * within(slab + dy, nslab)

                    @pl.when(ok == 1)
                    def _():
                        pltpu.make_async_remote_copy(
                            src, dst, send.at[e, i], recv.at[e, i], device_id=target, device_id_type=MESH).start()

        def arrive(e, ref):
            for i in range(8):
                @pl.when(alive[7 - i] == 1)
                def _():
                    hop(e, ref, i).wait_recv()

        def sent(e, ref):
            for i in range(8):
                @pl.when(alive[i] == 1)
                def _():
                    hop(e, ref, i).wait_send()

        zpos = lax.broadcasted_iota(jnp.int32, (rows, depth), 1)

        def reduce_columns(x, carry):
            s = st[x] * (1.0 - 0.5 * f_ext[W + x, 0:rows, :].astype(jnp.float32))
            low = jnp.where(zpos == 0, 0.0, pltpu.roll(s, 1, 1))
            high = jnp.where(zpos == depth - 1, 0.0, pltpu.roll(s, depth - 1, 1))
            up = 0.5 * (s + high)
            down = 0.5 * (s + low)
            a = jnp.where(zpos == 0, 0.0, down)
            c = jnp.where(zpos == depth - 1, 0.0, up)
            e = 0.001 * s + jnp.where(zpos == 0, down, 0.0) + jnp.where(zpos == depth - 1, up, 0.0)
            r = jnp.full((rows, depth), 0.001 / depth, jnp.float32)
            for level in range(levels):
                stride = 1 << level
                back = depth - stride
                recip = 1.0 / (a + c + e)
                al = a * pltpu.roll(recip, stride, 1)
                ga = c * pltpu.roll(recip, back, 1)
                alpha[level, x] = al
                gamma[level, x] = ga
                a = al * pltpu.roll(a, stride, 1)
                c = ga * pltpu.roll(c, back, 1)
                e = e + al * pltpu.roll(e, stride, 1) + ga * pltpu.roll(e, back, 1)
                r = r + al * pltpu.roll(r, stride, 1) + ga * pltpu.roll(r, back, 1)
            recip = 1.0 / e
            inv[x] = recip
            wts[x] = r * recip
            return carry

        zfull = lax.broadcasted_iota(jnp.int32, (ey, depth), 1)

        def faces(x, carry):
            k = k_ext[x]
            front = jnp.where(zfull == 0, 0.0, pltpu.roll(k, 1, 1))
            back = jnp.where(zfull == depth - 1, 0.0, pltpu.roll(k, depth - 1, 1))
            gzp = 0.5 * (k + back)
            gzm = 0.5 * (k + front)
            gyp = 0.5 * (k + pltpu.roll(k, ey - 1, 0))
            gym = 0.5 * (k + pltpu.roll(k, 1, 0))
            gxp = 0.5 * (k + k_ext[x + 1])
            gxm = 0.5 * (k + k_ext[x - 1])
            fl = f_ext[x].astype(jnp.float32)
            denom = gxp + gxm + gyp + gym + gzp + gzm + 1.0 - fl
            gx_[x] = gxp
            gy_[x] = gyp
            gz_[x] = jnp.where(zfull == depth - 1, 0.0, gzp)
            a_[x] = fl / denom
            return carry

        def all_faces():
            gx_[0] = 0.5 * (k_ext[0] + k_ext[1])
            lax.fori_loop(1, ex - 1, faces, 0, unroll=FACES)

        def relax(src, dst, level, width):
            def one(x, carry):
                here = src[x]
                gy = gy_[x]
                gz = gz_[x]
                total = s_ext[x] + gx_[x] * src[x + 1] + gx_[x - 1] * src[x - 1]
                total = total + gy * pltpu.roll(here, ey - 1, 0) + pltpu.roll(gy * here, 1, 0)
                total = total + gz * pltpu.roll(here, depth - 1, 1) + pltpu.roll(gz * here, 1, 1)
                value = a_[x] * total
                if width == ey:
                    dst[x] = value
                elif dst is fin_p:
                    dst[x - W] = value[0:width]
                else:
                    dst[x, 0:width] = value[0:width]
                return carry

            lax.fori_loop(level, ex - level, one, 0, unroll=ex - 2 * level)

        def first(x, carry):
            ta[x] = a_[x] * s_ext[x]
            return carry

        lane = lax.broadcasted_iota(jnp.int32, (rows, 128), 1)

        def mean_factor(held, base):
            comp = jnp.zeros((rows, 128), jnp.float32)
            for x in range(nx):
                part = wts[x] * (1.0 - held[base + x, 0:rows, :])
                comp = jnp.where(lane == x, jnp.sum(part, axis=1, keepdims=True), comp)
            return 1.0 + 0.3 * jnp.tanh(comp)

        st_away.wait_recv()
        st_keep.wait()
        const_arrive((0, 1))
        all_faces()
        const_arrive((2,))
        lax.fori_loop(1, ex - 1, first, 0, unroll=2)
        relax(ta, tb, 2, ey)
        relax(tb, ta, 3, ey)
        relax(ta, px0, 4, rows)
        push(0, px0)
        lax.fori_loop(0, nx, reduce_columns, 0, unroll=2)
        arrive(0, px0)
        relax(px0, ta, 1, ey)
        relax(ta, tb, 2, ey)
        relax(tb, ta, 3, ey)
        relax(ta, px1, 4, rows)

        factor = mean_factor(px1, W)
        cols[1, 0:rows, :] = factor
        push(2, cols)
        push(1, px1)
        sent(0, px0)
        arrive(2, cols)
        for x in range(ex):
            part, pos = (0, x + nx - W) if x < W else ((1, x - W) if x < W + nx else (2, x - W - nx))
            t = cols[part, :, pos:pos + 1]
            k_ext[x] = k_ext[x] * (t * t * t)
        all_faces()
        arrive(1, px1)
        relax(px1, ta, 1, ey)
        relax(ta, tb, 2, ey)
        relax(tb, ta, 3, ey)
        relax(ta, px2, 4, rows)
        push(3, px2)
        sent(2, cols)
        sent(1, px1)
        const_each(lambda c: c.wait_send(), None)
        st_away.wait_send()
        arrive(3, px2)
        relax(px2, ta, 1, ey)
        relax(ta, tb, 2, ey)
        relax(tb, ta, 3, ey)
        relax(ta, fin_p, 4, rows)

        def give(n, ref, dst, x0, xn):
            out = pltpu.make_async_remote_copy(
                ref.at[pl.ds(x0, xn), :, pl.ds(z_there, nz)], dst.at[pl.ds(x0, xn), pl.ds(mine, rows), :],
                psend.at[n], precv.at[n], device_id={"grp": other}, device_id_type=MESH)
            keep = pltpu.make_async_copy(
                ref.at[pl.ds(x0, xn), :, pl.ds(z_here, nz)], dst.at[pl.ds(x0, xn), pl.ds(mine, rows), :],
                loc.at[2 + n])
            return out, keep

        half = nx // 2
        gives = [give(1, fin_p, p_out, 0, nx), give(2, fin_d, d_out, 0, half), give(3, fin_d, d_out, half, half)]
        for c in gives[0]:
            c.start()

        def solve_columns(x, carry):
            r = 0.001 * (1.0 - fin_p[x])
            for level in range(levels):
                stride = 1 << level
                r = (r + alpha[level, x] * pltpu.roll(r, stride, 1)
                     + gamma[level, x] * pltpu.roll(r, depth - stride, 1))
            fin_d[x] = r * inv[x]
            return carry

        lax.fori_loop(0, nx, solve_columns, 0, unroll=nx)
        for n in range(2):
            for c in gives[1 + n]:
                c.start()

        factor = factor * mean_factor(fin_p, 0)
        spot = lane == lax.broadcasted_iota(jnp.int32, (rows, 128), 0) + g * rows
        pick = lax.broadcasted_iota(jnp.int32, (nx, 128), 0)
        mixed = jnp.zeros((nx, 128), jnp.float32)
        for x in range(nx):
            row = jnp.sum(jnp.where(spot, factor[:, x:x + 1], 0.0), axis=0, keepdims=True)
            mixed = jnp.where(pick == x, row, mixed)
        line[...] = mixed
        t_out = pltpu.make_async_remote_copy(
            line, line_in, psend.at[4], precv.at[4], device_id={"grp": other}, device_id_type=MESH)
        t_out.start()
        sent(3, px2)
        for out, keep in gives:
            out.wait_send()
            keep.wait()
        t_out.wait_send()
        t_out.wait_recv()
        th_out[...] = thick[...] * (mixed + line_in[...])[:, 0:ny]
        for out, keep in gives:
            out.wait_recv()

    return kernel, rows, depth, ex, ey, levels


def body(source, fill, material, thickness, perm_table, stiff_table):
    nx, ny, nz = source.shape
    kernel, rows, depth, ex, ey, levels = make_kernel(
        nx, ny, nz, lax.axis_size("gx"), lax.axis_size("gy"), perm_table.shape[0])
    f32, i32 = jnp.float32, jnp.int32
    vm = pl.BlockSpec(memory_space=pltpu.VMEM)
    hb = pl.BlockSpec(memory_space=pl.ANY)
    hbm = pl.BlockSpec(memory_space=pltpu.HBM)
    ext = pltpu.VMEM((ex, ey, depth), f32)
    iext = pltpu.VMEM((ex, ey, depth), i32)
    own = pltpu.VMEM((nx, rows, depth), f32)
    brick = pltpu.VMEM((nx, ny, nz), f32)
    dma = pltpu.SemaphoreType.DMA
    fields = pl.pallas_call(
        kernel,
        out_shape=(
            jax.ShapeDtypeStruct((nx, ny, nz), f32),
            jax.ShapeDtypeStruct((nx, ny, nz), f32),
            jax.ShapeDtypeStruct((nx, ny), f32),
        ),
        in_specs=[hbm] * 6,
        out_specs=(hb, hb, vm),
        scratch_shapes=[
            ext, iext, ext, ext, ext, ext, ext, ext, ext, ext, ext, ext,
            pltpu.VMEM((levels, nx, rows, depth), f32),
            pltpu.VMEM((levels, nx, rows, depth), f32),
            own, own,
            pltpu.VMEM((3, ey, 128), f32),
            own, own,
            pltpu.VMEM((nx, ny, nz), i32), brick, brick, own,
            pltpu.VMEM((nx, ny), f32),
            pltpu.VMEM((nx, 128), f32),
            pltpu.VMEM((nx, 128), f32),
            pltpu.SMEM(perm_table.shape, f32), pltpu.SMEM(stiff_table.shape, f32),
            dma((3, 2, 9)), dma((3, 2, 9)), dma((3, 2)),
            dma((4, 8)), dma((4, 8)), dma((5,)), dma((5,)), dma((8,)),
        ],
        compiler_params=pltpu.CompilerParams(
            collective_id=0, has_side_effects=True, vmem_limit_bytes=VMEM_LIMIT),
    )(*(pltpu.with_memory_space_constraint(a, pltpu.HBM)
        for a in (source, fill, material, thickness, perm_table, stiff_table)))

    def settle(*refs):
        ins, outs, sems = refs[:3], refs[3:6], refs[6]
        copies = [pltpu.make_async_copy(i, o, sems.at[n]) for n, (i, o) in enumerate(zip(ins, outs))]
        for c in copies:
            c.start()
        for c in copies:
            c.wait()

    return pl.pallas_call(
        settle,
        out_shape=tuple(jax.ShapeDtypeStruct(a.shape, f32) for a in fields),
        in_specs=[hb] * 3,
        out_specs=(hbm,) * 3,
        scratch_shapes=[dma((3,))],
        compiler_params=pltpu.CompilerParams(vmem_limit_bytes=1 << 20),
    )(*fields)


def solution(mesh):
    return jax.shard_map(
        body,
        mesh=mesh,
        in_specs=(
            P("gx", "gy", "grp"),
            P("gx", "gy", "grp"),
            P("gx", "gy", "grp"),
            P("gx", "gy"),
            P(),
            P(),
        ),
        out_specs=(P("gx", "gy", "grp"), P("gx", "gy", "grp"), P("gx", "gy")),
        check_vma=False,
    )
```

```python
import jax
import jax.numpy as jnp
from jax import lax
from jax.experimental import pallas as pl
from jax.experimental.pallas import tpu as pltpu
from jax.sharding import PartitionSpec as P

W = 4
VMEM_LIMIT = 24 << 20
MESH = pl.DeviceIdType.MESH
DIRS = [(-1, -1), (-1, 0), (-1, 1), (0, -1), (0, 1), (1, -1), (1, 0), (1, 1)]
NINE = [(0, 0)] + DIRS
ORDER = [0, 1, 2, 3, 4, 5, 6, 7]
FACES = 14


def spread(table, material, count):
    total = jnp.zeros(material.shape, jnp.float32)
    for entry in range(count):
        total = jnp.where(material == entry, table[entry], total)
    return total


def make_kernel(nx, ny, nz, ngx, ngy, mats):
    rows, depth = ny // 2, 2 * nz
    ex, ey = nx + 2 * W, rows + 2 * W
    nslab = 2 * ngy
    levels = depth.bit_length() - 1

    def blocks(dx, dy, reach):
        xr = reach - abs(dy)
        yr = reach - abs(dx)
        xs, xd = {-1: ((0, xr), (W + nx, xr)), 0: ((0, nx), (W, nx)), 1: ((nx - xr, xr), (W - xr, xr))}[dx]
        ys, yd = {-1: ((0, yr), (rows, yr)), 0: ((0, rows), (0, rows)),
                  1: ((rows - yr, yr), (ey - yr, yr))}[dy]
        return xs, ys, xd, yd

    def blocks_for(dx, dy, reach):
        _, (ys, yn), _, (yd, _) = blocks(0, dy, reach)
        xr = reach - abs(dy)
        yn, ys, yd = (yn, ys, yd) if dy == 0 else (reach - 1, ys + (1 if dy == 1 else 0), yd + (1 if dy == 1 else 0))
        xs = jnp.where(dx == -1, 0, nx - xr)
        xd = jnp.where(dx == -1, W + nx, W - xr)
        return (xs, xr), (ys, yn), (xd, xr), (yd, yn)

    def kernel(source, fill, material, thickness, perm_table, stiff_table, p_out, d_out, th_out,
               s_ext, f_ext, k_ext, px0, px1, px2, ta, tb, gx_, gy_, gz_, a_,
               alpha, gamma, inv, wts, cols, fin_p, fin_d, mat, kloc, stloc, st, thick, line, line_in, perm, stiffs,
               csend, crecv, cloc, send, recv, psend, precv, loc):
        g = lax.axis_index("grp")
        ix = lax.axis_index("gx")
        iy = lax.axis_index("gy")
        slab = 2 * iy + g
        far = jnp.where(lax.rem(ix, 4) < 2, -1, 1)
        long_way = jnp.where(lax.rem(ix, 4) == 0, 1, 0) + jnp.where(lax.rem(ix, 4) == 3, 1, 0)
        other = 1 - g

        def within(value, count):
            return jnp.where(value >= 0, 1, 0) * jnp.where(value < count, 1, 0)

        def place(dx, dy):
            x = jnp.clip(ix + dx, 0, ngx - 1)
            if dy == 0:
                return {"grp": g, "gx": x, "gy": iy}
            return {"grp": other, "gx": x, "gy": jnp.clip(iy + (g if dy == 1 else g - 1), 0, ngy - 1)}

        alive = [within(ix + dx, ngx) * within(slab + dy, nslab) for dx, dy in DIRS]

        barrier = pltpu.get_barrier_semaphore()
        for dx in (far, 0, -far):
            for dgy in (2 * g - 1, 0):
                for core in range(2):
                    ok = within(ix + dx, ngx) * within(iy + dgy, ngy)
                    if isinstance(dx, int) and isinstance(dgy, int):
                        ok = jnp.where(g == core, 0, 1)

                    @pl.when(ok == 1)
                    def _():
                        target = {"grp": core, "gx": jnp.clip(ix + dx, 0, ngx - 1),
                                  "gy": jnp.clip(iy + dgy, 0, ngy - 1)}
                        pl.semaphore_signal(barrier, 1, device_id=target, device_id_type=MESH)
        greeted = (sum(within(ix + dx, ngx) for dx in (-1, 0, 1))
                   * sum(within(2 * iy + j, nslab) for j in (-1, 0, 1, 2)) - 1)

        load_th = pltpu.make_async_copy(thickness, thick, loc.at[0])
        load_mat = pltpu.make_async_copy(material, mat, loc.at[1])
        load_perm = pltpu.make_async_copy(perm_table, perm, loc.at[6])
        load_stiff = pltpu.make_async_copy(stiff_table, stiffs, loc.at[7])
        for c in (load_th, load_mat, load_perm, load_stiff):
            c.start()

        for i in range(8):
            dx, dy = DIRS[i]
            _, _, (x0, xn), (y0, yn) = blocks(-dx, -dy, W)

            @pl.when(alive[i] == 0)
            def _():
                s_ext[x0:x0 + xn, y0:y0 + yn, :] = jnp.zeros((xn, yn, depth), jnp.float32)
                f_ext[x0:x0 + xn, y0:y0 + yn, :] = jnp.zeros((xn, yn, depth), jnp.int32)
                k_ext[x0:x0 + xn, y0:y0 + yn, :] = jnp.zeros((xn, yn, depth), jnp.float32)
                for ref in (px0, px1, px2):
                    ref[x0:x0 + xn, y0:y0 + yn, :] = jnp.zeros((xn, yn, depth), jnp.float32)
                cols[1 + dx, y0:y0 + yn, :] = jnp.zeros((yn, 128), jnp.float32)

        for c in (load_th, load_mat, load_perm, load_stiff):
            c.wait()
        diagonal = lax.broadcasted_iota(jnp.int32, (ny, ny), 0) == lax.broadcasted_iota(jnp.int32, (ny, ny), 1)
        for x in range(nx):
            across = jnp.broadcast_to(thick[x:x + 1, :], (ny, ny))
            t = jnp.sum(jnp.where(diagonal, across, 0.0), axis=1, keepdims=True)
            m = mat[x]
            kloc[x] = spread(perm, m, mats) * (t * t * t)
            stloc[x] = spread(stiffs, m, mats)

        pl.semaphore_wait(barrier, greeted)

        mine = pl.multiple_of(g * rows, rows)
        theirs = pl.multiple_of(other * rows, rows)
        z_here = pl.multiple_of(g * nz, nz)
        z_there = pl.multiple_of(other * nz, nz)
        consts = [(0, kloc, k_ext, W), (1, fill, f_ext, W - 1), (2, source, s_ext, W - 1)]

        def const_send(n, v, dx, dy, local=False):
            _, src, ext, reach = consts[n]
            if dx is None:
                (xs, xn), (ys, yn), (xd, _), (yd, _) = blocks(0, dy, reach)
                i, x = NINE.index((0, dy)), ix
            else:
                (xs, xn), (ys, yn), (xd, _), (yd, _) = blocks_for(dx, dy, reach)
                i, x = jnp.where(dx == -1, 2, 7) + dy, jnp.clip(ix + dx, 0, ngx - 1)
            core, dgy = (v + dy) % 2, (v + dy) // 2
            from_ = src.at[pl.ds(xs, xn), pl.ds(v * rows + ys, yn), :]
            to = ext.at[pl.ds(xd, xn), pl.ds(yd, yn), pl.ds(z_here, nz)]
            target = {"grp": core, "gx": x, "gy": jnp.clip(iy + dgy, 0, ngy - 1)}
            if local:
                return pltpu.make_async_copy(from_, to, cloc.at[n, 0 if dy == 0 else 1])
            return pltpu.make_async_remote_copy(
                from_, to, csend.at[n, v, i], crecv.at[n, g, i], device_id=target, device_id_type=MESH)

        def const_each(do_away, do_keep):
            for dx in (far, None, -far):
                for v in range(2):
                    for dy in (0, 1, -1):
                        core, dgy = (v + dy) % 2, (v + dy) // 2
                        if dx is None:
                            ok = within(iy + dgy, ngy)
                            if dgy == 0:
                                ok = jnp.where(g == core, 0, 1)
                                if do_keep is not None:
                                    @pl.when(g == core)
                                    def _():
                                        for n in range(3):
                                            do_keep(const_send(n, v, dx, dy, True))
                        else:
                            ok = within(ix + dx, ngx) * within(iy + dgy, ngy)

                        @pl.when(ok == 1)
                        def _():
                            for n in range(3):
                                do_away(const_send(n, v, dx, dy))

        def const_arrive(group):
            for src in range(2):
                for i in range(9):
                    dx, dy = NINE[i]
                    ok = within(ix - dx, ngx) * within(slab - dy, nslab)
                    if dx == 0:
                        here = jnp.where(g == src, 1, 0)
                        if dy == 1:
                            here = here * g
                        if dy == -1:
                            here = here * other
                        ok = ok * (1 - here)

                        @pl.when(here == 1)
                        def _():
                            for n in group:
                                _, ref, ext, reach = consts[n]
                                (xs, xn), (ys, yn), (xd, _), (yd, _) = blocks(dx, dy, reach)
                                pltpu.make_async_copy(
                                    ref.at[pl.ds(xs, xn), pl.ds(ys, yn), :],
                                    ext.at[pl.ds(xd, xn), pl.ds(yd, yn), pl.ds(src * nz, nz)],
                                    cloc.at[n, 0 if dy == 0 else 1]).wait()

                    @pl.when(ok == 1)
                    def _():
                        for n in group:
                            _, ref, ext, reach = consts[n]
                            (xs, xn), (ys, yn), (xd, _), (yd, _) = blocks(dx, dy, reach)
                            pltpu.make_async_remote_copy(
                                ref.at[pl.ds(xs, xn), pl.ds(ys, yn), :],
                                ext.at[pl.ds(xd, xn), pl.ds(yd, yn), pl.ds(src * nz, nz)],
                                csend.at[n, 0, i], crecv.at[n, src, i],
                                device_id={"grp": other}, device_id_type=MESH).wait_recv()

        st_away = pltpu.make_async_remote_copy(
            stloc.at[:, pl.ds(theirs, rows), :], st.at[:, :, pl.ds(z_here, nz)],
            psend.at[0], precv.at[0], device_id={"grp": other}, device_id_type=MESH)
        st_keep = pltpu.make_async_copy(
            stloc.at[:, pl.ds(mine, rows), :], st.at[:, :, pl.ds(z_here, nz)], loc.at[2])
        st_away.start()
        st_keep.start()
        const_each(lambda c: c.start(), lambda c: c.start())

        def hop(e, ref, i):
            dx, dy = DIRS[i]
            (xs, xn), (ys, yn), (xd, _), (yd, _) = blocks(dx, dy, W)
            if ref is cols:
                src = ref.at[1, pl.ds(ys, yn), :]
                dst = ref.at[1 - dx, pl.ds(yd, yn), :]
            else:
                src = ref.at[pl.ds(W + xs, xn), pl.ds(ys, yn), :]
                dst = ref.at[pl.ds(xd, xn), pl.ds(yd, yn), :]
            return pltpu.make_async_remote_copy(
                src, dst, send.at[e, i], recv.at[e, i], device_id=place(dx, dy), device_id_type=MESH)

        def push_one(e, ref, dx, dy, cond):
            if dx is None:
                (xs, xn), (ys, yn), (xd, _), (yd, _) = blocks(0, dy, W)
                i, x, into = DIRS.index((0, dy)), ix, 1
            else:
                (xs, xn), (ys, yn), (xd, _), (yd, _) = blocks_for(dx, dy, W)
                i, x, into = jnp.where(dx == -1, 1, 6) + dy, jnp.clip(ix + dx, 0, ngx - 1), 1 - dx
            if ref is cols:
                src, dst = ref.at[1, pl.ds(ys, yn), :], ref.at[into, pl.ds(yd, yn), :]
            else:
                src = ref.at[pl.ds(W + xs, xn), pl.ds(ys, yn), :]
                dst = ref.at[pl.ds(xd, xn), pl.ds(yd, yn), :]
            target = place(0, dy)
            target["gx"] = x
            ok = within(x if dx is None else ix + dx, ngx) * within(slab + dy, nslab) * cond

            @pl.when(ok == 1)
            def _():
                pltpu.make_async_remote_copy(
                    src, dst, send.at[e, i], recv.at[e, i], device_id=target, device_id_type=MESH).start()

        def push(e, ref, pause=None):
            for dy in (1, -1):
                push_one(e, ref, None, dy, 1)
            if pause:
                pause()
            for dy in (0, 1, -1):
                push_one(e, ref, far, dy, 1)
            for dy in (0, 1, -1):
                push_one(e, ref, -far, dy, 1)

        def arrive(e, ref):
            for i in range(8):
                @pl.when(alive[7 - i] == 1)
                def _():
                    hop(e, ref, i).wait_recv()

        def sent(e, ref):
            for i in range(8):
                @pl.when(alive[i] == 1)
                def _():
                    hop(e, ref, i).wait_send()

        zpos = lax.broadcasted_iota(jnp.int32, (rows, depth), 1)

        def reduce_columns(x, carry):
            s = st[x] * (1.0 - 0.5 * f_ext[W + x, 0:rows, :].astype(jnp.float32))
            low = jnp.where(zpos == 0, 0.0, pltpu.roll(s, 1, 1))
            high = jnp.where(zpos == depth - 1, 0.0, pltpu.roll(s, depth - 1, 1))
            up = 0.5 * (s + high)
            down = 0.5 * (s + low)
            a = jnp.where(zpos == 0, 0.0, down)
            c = jnp.where(zpos == depth - 1, 0.0, up)
            e = 0.001 * s + jnp.where(zpos == 0, down, 0.0) + jnp.where(zpos == depth - 1, up, 0.0)
            r = jnp.full((rows, depth), 0.001 / depth, jnp.float32)
            for level in range(levels):
                stride = 1 << level
                back = depth - stride
                recip = 1.0 / (a + c + e)
                al = a * pltpu.roll(recip, stride, 1)
                ga = c * pltpu.roll(recip, back, 1)
                alpha[level, x] = al
                gamma[level, x] = ga
                a = al * pltpu.roll(a, stride, 1)
                c = ga * pltpu.roll(c, back, 1)
                e = e + al * pltpu.roll(e, stride, 1) + ga * pltpu.roll(e, back, 1)
                r = r + al * pltpu.roll(r, stride, 1) + ga * pltpu.roll(r, back, 1)
            recip = 1.0 / e
            inv[x] = recip
            wts[x] = r * recip
            return carry

        zfull = lax.broadcasted_iota(jnp.int32, (ey, depth), 1)

        def faces(x, carry):
            k = k_ext[x]
            front = jnp.where(zfull == 0, 0.0, pltpu.roll(k, 1, 1))
            back = jnp.where(zfull == depth - 1, 0.0, pltpu.roll(k, depth - 1, 1))
            gzp = 0.5 * (k + back)
            gzm = 0.5 * (k + front)
            gyp = 0.5 * (k + pltpu.roll(k, ey - 1, 0))
            gym = 0.5 * (k + pltpu.roll(k, 1, 0))
            gxp = 0.5 * (k + k_ext[x + 1])
            gxm = 0.5 * (k + k_ext[x - 1])
            fl = f_ext[x].astype(jnp.float32)
            denom = gxp + gxm + gyp + gym + gzp + gzm + 1.0 - fl
            gx_[x] = gxp
            gy_[x] = gyp
            gz_[x] = jnp.where(zfull == depth - 1, 0.0, gzp)
            a_[x] = fl / denom
            return carry

        def all_faces():
            gx_[0] = 0.5 * (k_ext[0] + k_ext[1])
            lax.fori_loop(1, ex - 1, faces, 0, unroll=FACES)

        def relax(src, dst, level, width):
            def one(x, carry):
                here = src[x]
                gy = gy_[x]
                gz = gz_[x]
                total = s_ext[x] + gx_[x] * src[x + 1] + gx_[x - 1] * src[x - 1]
                total = total + gy * pltpu.roll(here, ey - 1, 0) + pltpu.roll(gy * here, 1, 0)
                total = total + gz * pltpu.roll(here, depth - 1, 1) + pltpu.roll(gz * here, 1, 1)
                value = a_[x] * total
                if width == ey:
                    dst[x] = value
                elif dst is fin_p:
                    dst[x - W] = value[0:width]
                else:
                    dst[x, 0:width] = value[0:width]
                return carry

            lax.fori_loop(level, ex - level, one, 0, unroll=ex - 2 * level)

        def first(x, carry):
            ta[x] = a_[x] * s_ext[x]
            return carry

        lane = lax.broadcasted_iota(jnp.int32, (rows, 128), 1)

        def mean_factor(held, base):
            comp = jnp.zeros((rows, 128), jnp.float32)
            for x in range(nx):
                part = wts[x] * (1.0 - held[base + x, 0:rows, :])
                comp = jnp.where(lane == x, jnp.sum(part, axis=1, keepdims=True), comp)
            return 1.0 + 0.3 * jnp.tanh(comp)

        st_away.wait_recv()
        st_keep.wait()
        const_arrive((0, 1))
        all_faces()
        const_arrive((2,))
        lax.fori_loop(1, ex - 1, first, 0, unroll=2)
        relax(ta, tb, 2, ey)
        relax(tb, ta, 3, ey)
        relax(ta, px0, 4, rows)
        push(0, px0)
        lax.fori_loop(0, nx, reduce_columns, 0, unroll=2)
        arrive(0, px0)
        relax(px0, ta, 1, ey)
        relax(ta, tb, 2, ey)
        relax(tb, ta, 3, ey)
        relax(ta, px1, 4, rows)

        held = []

        def columns():
            held.append(mean_factor(px1, W))
            cols[1, 0:rows, :] = held[0]
            push(2, cols)

        push(1, px1, columns)
        factor = held[0]
        sent(0, px0)
        arrive(2, cols)
        for x in range(ex):
            part, pos = (0, x + nx - W) if x < W else ((1, x - W) if x < W + nx else (2, x - W - nx))
            t = cols[part, :, pos:pos + 1]
            k_ext[x] = k_ext[x] * (t * t * t)
        all_faces()
        arrive(1, px1)
        relax(px1, ta, 1, ey)
        relax(ta, tb, 2, ey)
        relax(tb, ta, 3, ey)
        relax(ta, px2, 4, rows)
        push(3, px2)
        sent(2, cols)
        sent(1, px1)
        const_each(lambda c: c.wait_send(), None)
        st_away.wait_send()
        arrive(3, px2)
        relax(px2, ta, 1, ey)
        relax(ta, tb, 2, ey)
        relax(tb, ta, 3, ey)
        relax(ta, fin_p, 4, rows)

        def give(n, ref, dst, x0, xn):
            out = pltpu.make_async_remote_copy(
                ref.at[pl.ds(x0, xn), :, pl.ds(z_there, nz)], dst.at[pl.ds(x0, xn), pl.ds(mine, rows), :],
                psend.at[n], precv.at[n], device_id={"grp": other}, device_id_type=MESH)
            keep = pltpu.make_async_copy(
                ref.at[pl.ds(x0, xn), :, pl.ds(z_here, nz)], dst.at[pl.ds(x0, xn), pl.ds(mine, rows), :],
                loc.at[2 + n])
            return out, keep

        half = nx // 2
        gives = [give(1, fin_p, p_out, 0, nx), give(2, fin_d, d_out, 0, half), give(3, fin_d, d_out, half, half)]
        for c in gives[0]:
            c.start()

        def solve_columns(x, carry):
            r = 0.001 * (1.0 - fin_p[x])
            for level in range(levels):
                stride = 1 << level
                r = (r + alpha[level, x] * pltpu.roll(r, stride, 1)
                     + gamma[level, x] * pltpu.roll(r, depth - stride, 1))
            fin_d[x] = r * inv[x]
            return carry

        lax.fori_loop(0, nx, solve_columns, 0, unroll=nx)
        for n in range(2):
            for c in gives[1 + n]:
                c.start()

        factor = factor * mean_factor(fin_p, 0)
        spot = lane == lax.broadcasted_iota(jnp.int32, (rows, 128), 0) + g * rows
        pick = lax.broadcasted_iota(jnp.int32, (nx, 128), 0)
        mixed = jnp.zeros((nx, 128), jnp.float32)
        for x in range(nx):
            row = jnp.sum(jnp.where(spot, factor[:, x:x + 1], 0.0), axis=0, keepdims=True)
            mixed = jnp.where(pick == x, row, mixed)
        line[...] = mixed
        t_out = pltpu.make_async_remote_copy(
            line, line_in, psend.at[4], precv.at[4], device_id={"grp": other}, device_id_type=MESH)
        t_out.start()
        sent(3, px2)
        for out, keep in gives:
            out.wait_send()
            keep.wait()
        t_out.wait_send()
        t_out.wait_recv()
        th_out[...] = thick[...] * (mixed + line_in[...])[:, 0:ny]
        for out, keep in gives:
            out.wait_recv()

    return kernel, rows, depth, ex, ey, levels


def body(source, fill, material, thickness, perm_table, stiff_table):
    nx, ny, nz = source.shape
    kernel, rows, depth, ex, ey, levels = make_kernel(
        nx, ny, nz, lax.axis_size("gx"), lax.axis_size("gy"), perm_table.shape[0])
    f32, i32 = jnp.float32, jnp.int32
    vm = pl.BlockSpec(memory_space=pltpu.VMEM)
    hb = pl.BlockSpec(memory_space=pl.ANY)
    hbm = pl.BlockSpec(memory_space=pltpu.HBM)
    ext = pltpu.VMEM((ex, ey, depth), f32)
    iext = pltpu.VMEM((ex, ey, depth), i32)
    own = pltpu.VMEM((nx, rows, depth), f32)
    brick = pltpu.VMEM((nx, ny, nz), f32)
    dma = pltpu.SemaphoreType.DMA
    fields = pl.pallas_call(
        kernel,
        out_shape=(
            jax.ShapeDtypeStruct((nx, ny, nz), f32),
            jax.ShapeDtypeStruct((nx, ny, nz), f32),
            jax.ShapeDtypeStruct((nx, ny), f32),
        ),
        in_specs=[hbm] * 6,
        out_specs=(hb, hb, vm),
        scratch_shapes=[
            ext, iext, ext, ext, ext, ext, ext, ext, ext, ext, ext, ext,
            pltpu.VMEM((levels, nx, rows, depth), f32),
            pltpu.VMEM((levels, nx, rows, depth), f32),
            own, own,
            pltpu.VMEM((3, ey, 128), f32),
            own, own,
            pltpu.VMEM((nx, ny, nz), i32), brick, brick, own,
            pltpu.VMEM((nx, ny), f32),
            pltpu.VMEM((nx, 128), f32),
            pltpu.VMEM((nx, 128), f32),
            pltpu.SMEM(perm_table.shape, f32), pltpu.SMEM(stiff_table.shape, f32),
            dma((3, 2, 9)), dma((3, 2, 9)), dma((3, 2)),
            dma((4, 8)), dma((4, 8)), dma((5,)), dma((5,)), dma((8,)),
        ],
        compiler_params=pltpu.CompilerParams(
            collective_id=0, has_side_effects=True, vmem_limit_bytes=VMEM_LIMIT),
    )(*(pltpu.with_memory_space_constraint(a, pltpu.HBM)
        for a in (source, fill, material, thickness, perm_table, stiff_table)))

    def settle(*refs):
        ins, outs, sems = refs[:3], refs[3:6], refs[6]
        copies = [pltpu.make_async_copy(i, o, sems.at[n]) for n, (i, o) in enumerate(zip(ins, outs))]
        for c in copies:
            c.start()
        for c in copies:
            c.wait()

    return pl.pallas_call(
        settle,
        out_shape=tuple(jax.ShapeDtypeStruct(a.shape, f32) for a in fields),
        in_specs=[hb] * 3,
        out_specs=(hbm,) * 3,
        scratch_shapes=[dma((3,))],
        compiler_params=pltpu.CompilerParams(vmem_limit_bytes=1 << 20),
    )(*fields)


def solution(mesh):
    return jax.shard_map(
        body,
        mesh=mesh,
        in_specs=(
            P("gx", "gy", "grp"),
            P("gx", "gy", "grp"),
            P("gx", "gy", "grp"),
            P("gx", "gy"),
            P(),
            P(),
        ),
        out_specs=(P("gx", "gy", "grp"), P("gx", "gy", "grp"), P("gx", "gy")),
        check_vma=False,
    )
```
